128 devices in a mesh: row: 16 (over y, z), col: 8 (over x, core).
Axes of the slice: x: 4, y: 4, z: 4, core: 2. Of those that a mesh axis runs over, the one named last changes fastest.
Arguments:
- init_mean: float32 [256], replicated, may hold values from -6 to 6
- init_var: float32 [256], replicated, may hold values from 0.1 to 2
- decay: float32 [4096, 256], P(('row', 'col')), may hold values from 0 to 1
- coupling: bfloat16 [4096, 256, 256], P(('row', 'col')), may hold values from -0.0234375 to 0.0234375
- obs_map: bfloat16 [4096, 64, 256], P(('row', 'col')), may hold values from -0.375 to 0.375
- gain: bfloat16 [4096, 64, 256], P(('row', 'col')), may hold values from -0.0625 to 0.0625
- noise_factor: bfloat16 [256, 256], replicated, may hold values from -0.02734375 to 0.02734375
- obs_var: float32 [64], replicated, may hold values from 0.25 to 4
- observed: float32 [4096, 64], P(('row', 'col')), may hold values from -6 to 6
Outputs:
- means: float32 [4096, 256], P(('row', 'col'))
- variances: float32 [4096, 256], P(('row', 'col'))
The draws below stay inside these ranges and needn't reach their ends.
All inputs are finite; a program needn't handle non-finite values.
Results may differ from the reference program's by a relative error of at most 0.00037.
Values sent between devices are 32-bit elements; how exact they have to be, the bound alone decides.
A program may use at most 128 MiB of HBM per device.

```python
import math
import jax
import jax.numpy as jnp
from jax import lax

S = 256
M = 64
STEPS_DEV = 32
T_STEPS = 4096


def draw_decay(key, part):
    subkeys = jax.random.split(jax.random.fold_in(key, 11), 7)
    slow_share = 0.5
    chooser = jax.random.uniform(subkeys[0], (S,), jnp.float32)
    slowly = chooser < slow_share
    slow_rate = jnp.exp(jax.random.uniform(subkeys[1], (S,), jnp.float32, math.log(0.05), math.log(1.0))) / T_STEPS
    fast_rate = 1.0 / jax.random.uniform(subkeys[2], (S,), jnp.float32, 30.0, 50.0)
    rates = jnp.where(slowly, slow_rate, fast_rate)
    factor = jnp.exp(jax.random.uniform(subkeys[3], (T_STEPS // STEPS_DEV, 1), jnp.float32, math.log(0.5), math.log(2.0)))
    factor = jnp.repeat(factor, STEPS_DEV, axis=0)
    jitter = jax.random.uniform(subkeys[4], (T_STEPS, S), jnp.float32, 0.5, 1.5)
    base = jnp.exp(-rates[None, :] * factor * jitter)
    spots = jax.random.randint(subkeys[5], (3,), 0, T_STEPS)
    struck = jnp.any(jnp.arange(T_STEPS)[:, None] == spots[None, :], axis=1)
    losses = jax.random.uniform(subkeys[6], (T_STEPS, S), jnp.float32, 0.6, 0.85)
    return jnp.where(struck[:, None] & slowly[None, :], base * losses, base)


def levels(own_key, dims, shards, low, high):
    level = 1.0
    for dim, parts in shards:
        draws = jax.random.uniform(jax.random.fold_in(jax.random.fold_in(own_key, 6), dim), (parts,), jnp.float32, low / len(shards), high / len(shards))
        level = level * jnp.repeat(jnp.exp(draws), dims[dim] // parts).reshape((-1,) + (1,) * (len(dims) - 1 - dim))
    return level


def centred(stream_key, dims, deviation, limit, cuts=(), held_as=jnp.bfloat16):
    entries = deviation * jax.random.normal(stream_key, dims, jnp.float32)
    if cuts:
        entries = entries * levels(stream_key, dims, cuts, -0.22, 0.18)
    return jnp.clip(entries, -limit, limit).astype(held_as)


def setup_inputs(seed: int = 0) -> dict:
    splits = jax.random.split(jax.random.key(seed), 10)
    init_mean = centred(splits[0], (S,), 1.0, 6.0, (), jnp.float32)
    init_var = jnp.clip(jnp.exp(jax.random.uniform(splits[1], (S,), jnp.float32, math.log(0.1), math.log(2.0))), 0.1, 2.0)
    decay = draw_decay(jax.random.fold_in(splits[9], 71), 0)
    coupling = centred(splits[3], (T_STEPS, S, S), (0.025 * S ** -0.5), 0.0234375, ((0, 128),))
    obs_map = centred(splits[4], (T_STEPS, M, S), S ** -0.5, 0.375, ((0, 128),))
    gain = centred(splits[5], (T_STEPS, M, S), (0.032 * M ** -0.5), 0.0625, ((0, 128),))
    noise_factor = centred(splits[6], (S, S), (0.03 * S ** -0.5), 0.02734375)
    obs_var = jnp.clip(jnp.exp(jax.random.uniform(splits[7], (M,), jnp.float32, math.log(0.25), math.log(4.0))), 0.25, 4.0)
    observed = centred(splits[8], (T_STEPS, M), 1.0, 6.0, ((0, 128),), jnp.float32)
    return {"init_mean": init_mean, "init_var": init_var, "decay": decay, "coupling": coupling, "obs_map": obs_map, "gain": gain, "noise_factor": noise_factor, "obs_var": obs_var, "observed": observed}


highest = lax.Precision.HIGHEST


def build(decay_t, coupling_t, obs_map_t, gain_t, noise_factor, obs_var, observed_t):
    trans = jnp.diag(decay_t) + coupling_t.astype(jnp.float32)
    obs_f = obs_map_t.astype(jnp.float32) * decay_t[None, :] + jnp.dot(obs_map_t, coupling_t, preferred_element_type=jnp.float32)
    obs_f = obs_f.astype(jnp.bfloat16)
    gain_trans = gain_t.T
    step_map = trans - jnp.dot(gain_trans, obs_f, preferred_element_type=jnp.float32)
    obs_g = jnp.dot(obs_map_t, noise_factor, preferred_element_type=jnp.float32).astype(jnp.bfloat16)
    shaped = noise_factor.astype(jnp.float32) - jnp.dot(gain_trans, obs_g, preferred_element_type=jnp.float32)
    shaped = shaped.astype(jnp.bfloat16)
    weighted = (gain_t.astype(jnp.float32) * obs_var[:, None]).astype(jnp.bfloat16)
    noise = jnp.dot(shaped, shaped.T, preferred_element_type=jnp.float32) + jnp.dot(gain_trans, weighted, preferred_element_type=jnp.float32)
    shift = jnp.dot(observed_t, gain_t.astype(jnp.float32), precision=highest)
    return step_map, shift, noise


def reference(init_mean, init_var, decay, coupling, obs_map, gain, noise_factor, obs_var, observed):
    def advance(carry, inputs):
        state_mean, state_cov = carry
        decay_t, coupling_t, obs_map_t, gain_t, observed_t = inputs
        step_map, shift, noise = build(decay_t, coupling_t, obs_map_t, gain_t, noise_factor, obs_var, observed_t)
        state_mean = jnp.dot(step_map, state_mean, precision=highest) + shift
        state_cov = jnp.dot(jnp.dot(step_map, state_cov, precision=highest), step_map.T, precision=highest) + noise
        return (state_mean, state_cov), (state_mean, jnp.diagonal(state_cov))

    start = (init_mean, jnp.diag(init_var))
    _, (means, variances) = lax.scan(advance, start, (decay, coupling, obs_map, gain, observed))
    return means, variances
```

```python
import functools

import jax
import jax.numpy as jnp
from jax import lax
from jax.experimental import pallas as pl
from jax.experimental.pallas import tpu as pltpu
from jax.sharding import PartitionSpec as P

highest = lax.Precision.HIGHEST
f32 = jnp.float32
bf16 = jnp.bfloat16
PAD = 16
SPB = 4


def dot_nn(a, b):
    return lax.dot_general(a, b, (((1,), (0,)), ((), ())), preferred_element_type=f32)


def dot_nt(a, b):
    return lax.dot_general(a, b, (((1,), (1,)), ((), ())), preferred_element_type=f32)


def split(x):
    hi = x.astype(bf16)
    return hi, (x - hi.astype(f32)).astype(bf16)


def eye(n):
    row = lax.broadcasted_iota(jnp.int32, (n, n), 0)
    col = lax.broadcasted_iota(jnp.int32, (n, n), 1)
    return row == col


def local_kernel(steps, decay_ref, observed_ref, var_ref, coupling_ref, map_ref, gain_ref,
                 factor_ref, hi_ref, lo_ref, diag_ref, shift_ref, total_ref,
                 state, e_hi, e_lo, noise, shift):
    i = pl.program_id(0)
    s = decay_ref.shape[1]
    put = lax.rem(i, 2)
    get = 1 - put

    @pl.when(i <= 1)
    def _():
        unit = jnp.where(eye(s), 1.0, 0.0).astype(f32)
        state[...] = jnp.concatenate([unit, jnp.zeros((s + PAD, s), f32)], axis=0)

    factor = factor_ref[...]
    block = jnp.minimum(i, pl.num_programs(0) - 2)
    for j in range(steps):
        t = block * steps + j
        decay = decay_ref[pl.ds(t, 1), :]
        obs_map = map_ref[j]
        gain = gain_ref[j]
        coupling = coupling_ref[j]
        gain_t = gain.T
        obs_f = (obs_map.astype(f32) * decay + dot_nn(obs_map, coupling)).astype(bf16)
        obs_g = dot_nn(obs_map, factor).astype(bf16)
        e = coupling.astype(f32) - dot_nn(gain_t, obs_f)
        hi, lo = split(e)
        e_hi[put, j] = hi
        e_lo[put, j] = lo
        shaped = (factor.astype(f32) - dot_nn(gain_t, obs_g)).astype(bf16)
        weighted = (gain.astype(f32) * var_ref[...]).astype(bf16)
        noise[put, j] = dot_nt(shaped, shaped) + dot_nn(gain_t, weighted)
        z_hi, z_lo = split(jnp.broadcast_to(observed_ref[pl.ds(t, 1), :], (PAD, gain.shape[0])))
        shift[put, j] = dot_nn(z_hi, gain) + dot_nn(z_lo, gain)

    block = jnp.maximum(i - 1, 0)
    diagonal = eye(s)
    x = state[...]
    for j in range(steps):
        t = block * steps + j
        decay = decay_ref[pl.ds(t, 1), :]
        decay_t = jnp.broadcast_to(decay, (8, s)).T[:, 0:1]
        eh, el = e_hi[get, j], e_lo[get, j]
        x_hi, x_lo = split(x)
        y = x * decay + (dot_nt(x_hi, eh) + (dot_nt(x_lo, eh) + dot_nt(x_hi, el)))
        maps, v, b = y[:s], y[s:2 * s], y[2 * s:]
        m_hi, m_lo = split(maps)
        hi_ref[j] = m_hi
        lo_ref[j] = m_lo
        v_hi, v_lo = split(v)
        n = v * decay_t + noise[get, j] + (dot_nn(eh, v_hi) + (dot_nn(eh, v_lo) + dot_nn(el, v_hi)))
        b = b + shift[get, j]
        diag_ref[pl.ds(t, 1), :] = jnp.sum(jnp.where(diagonal, n, 0.0), axis=0, keepdims=True)
        shift_ref[pl.ds(t, 1), :] = b[0:1]
        x = jnp.concatenate([maps, n, b], axis=0)
    state[...] = x

    @pl.when(i == pl.num_programs(0) - 1)
    def _():
        total_ref[...] = x


def local_prefix(decay, coupling, obs_map, gain, factor, obs_var, observed):
    count, s = decay.shape
    m = obs_map.shape[1]
    steps = SPB
    blocks = count // steps
    ahead = lambda i: (jnp.minimum(i, blocks - 1), 0, 0)
    behind = lambda i: (jnp.maximum(i - 1, 0), 0, 0)
    whole = lambda i: (0, 0)
    return pl.pallas_call(
        functools.partial(local_kernel, steps),
        grid=(blocks + 1,),
        in_specs=[
            pl.BlockSpec((count, s), whole),
            pl.BlockSpec((count, m), whole),
            pl.BlockSpec((m, 1), whole),
            pl.BlockSpec((steps, s, s), ahead),
            pl.BlockSpec((steps, m, s), ahead),
            pl.BlockSpec((steps, m, s), ahead),
            pl.BlockSpec((s, s), whole),
        ],
        out_specs=[
            pl.BlockSpec((steps, s, s), behind),
            pl.BlockSpec((steps, s, s), behind),
            pl.BlockSpec((count, s), whole),
            pl.BlockSpec((count, s), whole),
            pl.BlockSpec((2 * s + PAD, s), whole),
        ],
        out_shape=[
            jax.ShapeDtypeStruct((count, s, s), bf16),
            jax.ShapeDtypeStruct((count, s, s), bf16),
            jax.ShapeDtypeStruct((count, s), f32),
            jax.ShapeDtypeStruct((count, s), f32),
            jax.ShapeDtypeStruct((2 * s + PAD, s), f32),
        ],
        scratch_shapes=[
            pltpu.VMEM((2 * s + PAD, s), f32),
            pltpu.VMEM((2, steps, s, s), bf16),
            pltpu.VMEM((2, steps, s, s), bf16),
            pltpu.VMEM((2, steps, s, s), f32),
            pltpu.VMEM((2, steps, PAD, s), f32),
        ],
        name="local_prefix",
    )(decay, observed, obs_var[:, None], coupling, obs_map, gain, factor)


def output_kernel(steps, entry_ref, hi_ref, lo_ref, diag_ref, shift_ref, mean_ref, var_ref, left):
    i = pl.program_id(0)
    s = hi_ref.shape[2]
    rows = s + PAD

    @pl.when(i == 0)
    def _():
        hi, lo = split(entry_ref[...])
        left[:rows] = hi
        left[rows:] = lo

    for j in range(steps):
        t = i * steps + j
        hi, lo = hi_ref[j], lo_ref[j]
        both = dot_nn(left[...], hi)
        r = both[:rows] + (both[rows:] + dot_nn(left[:rows], lo))
        maps = hi.astype(f32) + lo.astype(f32)
        var_ref[pl.ds(t, 1), :] = (
            jnp.sum(r[:s] * maps, axis=0, keepdims=True) + diag_ref[pl.ds(t, 1), :]
        )
        mean_ref[pl.ds(t, 1), :] = r[s:s + 1] + shift_ref[pl.ds(t, 1), :]


def outputs(entry, hi, lo, diag, shift):
    count, s = diag.shape
    steps = SPB
    whole = lambda i: (0, 0)
    return pl.pallas_call(
        functools.partial(output_kernel, steps),
        grid=(count // steps,),
        in_specs=[
            pl.BlockSpec((s + PAD, s), whole),
            pl.BlockSpec((steps, s, s), lambda i: (i, 0, 0)),
            pl.BlockSpec((steps, s, s), lambda i: (i, 0, 0)),
            pl.BlockSpec((count, s), whole),
            pl.BlockSpec((count, s), whole),
        ],
        out_specs=[pl.BlockSpec((count, s), whole), pl.BlockSpec((count, s), whole)],
        out_shape=[jax.ShapeDtypeStruct((count, s), f32)] * 2,
        scratch_shapes=[pltpu.VMEM((2 * (s + PAD), s), bf16)],
        name="outputs",
    )(entry, hi, lo, diag, shift)


def entering(shard, axis, combine, identity):
    size, place = (lax.axis_size(axis), lax.axis_index(axis))
    everything = jax.tree.map(lambda part: lax.all_gather(part, axis), shard)
    start = jax.tree.map(
        lambda part, zero: jnp.broadcast_to(jnp.asarray(zero, part.dtype), part.shape),
        shard,
        identity,
    )

    def hop(k, before):
        reached = k < place
        new = combine(before, jax.tree.map(lambda part: part[k], everything))
        return jax.tree.map(lambda a, b: jnp.where(reached, a, b), new, before)

    return lax.fori_loop(0, size, hop, start)


def broadcast(block, axis, holder):
    block = jnp.where(lax.axis_index(axis) == holder, block, jnp.zeros_like(block))
    return lax.psum(block, axis)


def combine(earlier, later):
    earlier_map, earlier_shift, earlier_noise = earlier
    later_map, later_shift, later_noise = later
    joined_map = jnp.matmul(later_map, earlier_map, precision=highest)
    joined_shift = jnp.einsum("ij,j->i", later_map, earlier_shift, precision=highest) + later_shift
    moved = jnp.matmul(later_map, earlier_noise, precision=highest)
    joined_noise = jnp.matmul(moved, later_map.T, precision=highest) + later_noise
    return (joined_map, joined_shift, joined_noise)


def entry_of(total, init_mean, init_var):
    s = init_mean.shape[0]
    neutral = (jnp.eye(s, dtype=f32), jnp.zeros((s,), f32), jnp.zeros((s, s), f32))
    element = (total[:s].T, total[2 * s], total[s:2 * s])
    inner = entering(element, "col", combine, neutral)
    row_whole = combine(inner, element)
    row_total = tuple(broadcast(part, "col", lax.axis_size("col") - 1) for part in row_whole)
    outer = entering(row_total, "row", combine, neutral)
    carry_map, carry_shift, carry_noise = combine(outer, inner)
    mean = jnp.dot(carry_map, init_mean, precision=highest) + carry_shift
    cov = jnp.dot(carry_map * init_var[None, :], carry_map.T, precision=highest) + carry_noise
    return jnp.concatenate([cov, jnp.broadcast_to(mean, (PAD, s))], axis=0)


def per_device(
    init_mean, init_var, decay, coupling, obs_map, gain, noise_factor, obs_var, observed
):
    hi, lo, diag, shift, total = local_prefix(
        decay, coupling, obs_map, gain, noise_factor, obs_var, observed
    )
    entry = entry_of(total, init_mean, init_var)
    means, variances = outputs(entry, hi, lo, diag, shift)
    return (means, variances)


def solution(mesh):
    return jax.shard_map(
        per_device,
        mesh=mesh,
        in_specs=(
            P(),
            P(),
            P(("row", "col"), None),
            P(("row", "col"), None, None),
            P(("row", "col"), None, None),
            P(("row", "col"), None, None),
            P(),
            P(),
            P(("row", "col"), None),
        ),
        out_specs=(P(("row", "col"), None), P(("row", "col"), None)),
        check_vma=False,
    )
```

```python
import functools

import jax
import jax.numpy as jnp
from jax import lax
from jax.experimental import pallas as pl
from jax.experimental.pallas import tpu as pltpu
from jax.sharding import PartitionSpec as P

f32 = jnp.float32
bf16 = jnp.bfloat16
PAD = 16
SPB = 4


def dot_nn(a, b):
    return lax.dot_general(a, b, (((1,), (0,)), ((), ())), preferred_element_type=f32)


def dot_nt(a, b):
    return lax.dot_general(a, b, (((1,), (1,)), ((), ())), preferred_element_type=f32)


def split(x):
    hi = x.astype(bf16)
    return hi, (x - hi.astype(f32)).astype(bf16)


def eye(n):
    row = lax.broadcasted_iota(jnp.int32, (n, n), 0)
    col = lax.broadcasted_iota(jnp.int32, (n, n), 1)
    return row == col


def local_kernel(steps, decay_ref, observed_ref, var_ref, coupling_ref, map_ref, gain_ref,
                 factor_ref, hi_ref, lo_ref, diag_ref, shift_ref, total_ref,
                 state, e_hi, e_lo, noise, shift):
    i = pl.program_id(0)
    s = decay_ref.shape[1]
    put = lax.rem(i, 2)
    get = 1 - put

    @pl.when(i <= 1)
    def _():
        unit = jnp.where(eye(s), 1.0, 0.0).astype(f32)
        state[...] = jnp.concatenate([unit, jnp.zeros((s + PAD, s), f32)], axis=0)

    factor = factor_ref[...]
    block = jnp.minimum(i, pl.num_programs(0) - 2)
    for j in range(steps):
        t = block * steps + j
        decay = decay_ref[pl.ds(t, 1), :]
        obs_map = map_ref[j]
        gain = gain_ref[j]
        coupling = coupling_ref[j]
        gain_t = gain.T
        obs_f = (obs_map.astype(f32) * decay + dot_nn(obs_map, coupling)).astype(bf16)
        obs_g = dot_nn(obs_map, factor).astype(bf16)
        e = coupling.astype(f32) - dot_nn(gain_t, obs_f)
        hi, lo = split(e)
        e_hi[put, j] = hi
        e_lo[put, j] = lo
        shaped = (factor.astype(f32) - dot_nn(gain_t, obs_g)).astype(bf16)
        weighted = (gain.astype(f32) * var_ref[...]).astype(bf16)
        noise[put, j] = dot_nt(shaped, shaped) + dot_nn(gain_t, weighted)
        z_hi, z_lo = split(jnp.broadcast_to(observed_ref[pl.ds(t, 1), :], (PAD, gain.shape[0])))
        shift[put, j] = dot_nn(z_hi, gain) + dot_nn(z_lo, gain)

    block = jnp.maximum(i - 1, 0)
    diagonal = eye(s)
    x = state[...]
    for j in range(steps):
        t = block * steps + j
        decay = decay_ref[pl.ds(t, 1), :]
        decay_t = jnp.broadcast_to(decay, (8, s)).T[:, 0:1]
        eh, el = e_hi[get, j], e_lo[get, j]
        x_hi, x_lo = split(x)
        y = x * decay + (dot_nt(x_hi, eh) + (dot_nt(x_lo, eh) + dot_nt(x_hi, el)))
        maps, v, b = y[:s], y[s:2 * s], y[2 * s:]
        m_hi, m_lo = split(maps)
        hi_ref[j] = m_hi
        lo_ref[j] = m_lo
        v_hi, v_lo = split(v)
        n = v * decay_t + noise[get, j] + (dot_nn(eh, v_hi) + (dot_nn(eh, v_lo) + dot_nn(el, v_hi)))
        b = b + shift[get, j]
        diag_ref[pl.ds(t, 1), :] = jnp.sum(jnp.where(diagonal, n, 0.0), axis=0, keepdims=True)
        shift_ref[pl.ds(t, 1), :] = b[0:1]
        x = jnp.concatenate([maps, n, b], axis=0)
    state[...] = x

    @pl.when(i == pl.num_programs(0) - 1)
    def _():
        total_ref[...] = x


def local_prefix(decay, coupling, obs_map, gain, factor, obs_var, observed):
    count, s = decay.shape
    m = obs_map.shape[1]
    steps = SPB
    blocks = count // steps
    ahead = lambda i: (jnp.minimum(i, blocks - 1), 0, 0)
    behind = lambda i: (jnp.maximum(i - 1, 0), 0, 0)
    whole = lambda i: (0, 0)
    return pl.pallas_call(
        functools.partial(local_kernel, steps),
        grid=(blocks + 1,),
        in_specs=[
            pl.BlockSpec((count, s), whole),
            pl.BlockSpec((count, m), whole),
            pl.BlockSpec((m, 1), whole),
            pl.BlockSpec((steps, s, s), ahead),
            pl.BlockSpec((steps, m, s), ahead),
            pl.BlockSpec((steps, m, s), ahead),
            pl.BlockSpec((s, s), whole),
        ],
        out_specs=[
            pl.BlockSpec((steps, s, s), behind),
            pl.BlockSpec((steps, s, s), behind),
            pl.BlockSpec((count, s), whole),
            pl.BlockSpec((count, s), whole),
            pl.BlockSpec((2 * s + PAD, s), whole),
        ],
        out_shape=[
            jax.ShapeDtypeStruct((count, s, s), bf16),
            jax.ShapeDtypeStruct((count, s, s), bf16),
            jax.ShapeDtypeStruct((count, s), f32),
            jax.ShapeDtypeStruct((count, s), f32),
            jax.ShapeDtypeStruct((2 * s + PAD, s), f32),
        ],
        scratch_shapes=[
            pltpu.VMEM((2 * s + PAD, s), f32),
            pltpu.VMEM((2, steps, s, s), bf16),
            pltpu.VMEM((2, steps, s, s), bf16),
            pltpu.VMEM((2, steps, s, s), f32),
            pltpu.VMEM((2, steps, PAD, s), f32),
        ],
        name="local_prefix",
    )(decay, observed, obs_var[:, None], coupling, obs_map, gain, factor)


def output_kernel(steps, entry_ref, hi_ref, lo_ref, diag_ref, shift_ref, mean_ref, var_ref, left):
    i = pl.program_id(0)
    s = hi_ref.shape[2]
    rows = s + PAD

    @pl.when(i == 0)
    def _():
        hi, lo = split(entry_ref[...])
        left[:rows] = hi
        left[rows:] = lo

    for j in range(steps):
        t = i * steps + j
        hi, lo = hi_ref[j], lo_ref[j]
        both = dot_nn(left[...], hi)
        r = both[:rows] + (both[rows:] + dot_nn(left[:rows], lo))
        maps = hi.astype(f32) + lo.astype(f32)
        var_ref[pl.ds(t, 1), :] = (
            jnp.sum(r[:s] * maps, axis=0, keepdims=True) + diag_ref[pl.ds(t, 1), :]
        )
        mean_ref[pl.ds(t, 1), :] = r[s:s + 1] + shift_ref[pl.ds(t, 1), :]


def outputs(entry, hi, lo, diag, shift):
    count, s = diag.shape
    steps = SPB
    whole = lambda i: (0, 0)
    return pl.pallas_call(
        functools.partial(output_kernel, steps),
        grid=(count // steps,),
        in_specs=[
            pl.BlockSpec((s + PAD, s), whole),
            pl.BlockSpec((steps, s, s), lambda i: (i, 0, 0)),
            pl.BlockSpec((steps, s, s), lambda i: (i, 0, 0)),
            pl.BlockSpec((count, s), whole),
            pl.BlockSpec((count, s), whole),
        ],
        out_specs=[pl.BlockSpec((count, s), whole), pl.BlockSpec((count, s), whole)],
        out_shape=[jax.ShapeDtypeStruct((count, s), f32)] * 2,
        scratch_shapes=[pltpu.VMEM((2 * (s + PAD), s), bf16)],
        name="outputs",
    )(entry, hi, lo, diag, shift)


MESH_ID = pl.DeviceIdType.MESH


def join(first, later, lead):
    s = later.shape[1]
    t_hi, t_lo = split(later[:s])
    x_hi, x_lo = split(first)
    y = dot_nn(x_hi, t_hi) + (dot_nn(x_lo, t_hi) + dot_nn(x_hi, t_lo))
    v_hi, v_lo = split(y[lead:lead + s])
    u_hi, u_lo = t_hi.T, t_lo.T
    n = dot_nn(u_hi, v_hi) + (dot_nn(u_hi, v_lo) + dot_nn(u_lo, v_hi)) + later[s:2 * s]
    b = y[lead + s:] + later[2 * s:]
    parts = [y[:lead], n, b] if lead else [n, b]
    return jnp.concatenate(parts, axis=0)


def scan_kernel(total_ref, mean_ref, var_ref, entry_ref, all_x, all_z, all_y, before_x, before_z,
                chain, pair, state, send_sem, recv_sem, pair_sem, state_sem):
    row, col = lax.axis_index("row"), lax.axis_index("col")
    y, z = row // 4, lax.rem(row, 4)
    x, core = col // 2, lax.rem(col, 2)
    s = total_ref.shape[1]
    half = total_ref.shape[0] // 2
    upper, lower = pl.ds(0, half), pl.ds(half, half)

    def step(p, by):
        return lax.rem(p + by, 4)

    def along_x(by):
        return (row, step(x, by) * 2 + core)

    def along_z(by):
        return (y * 4 + step(z, by), col)

    def along_y(by):
        return (step(y, by) * 4 + z, col)

    partner = (row, x * 2 + 1 - core)
    barrier = pltpu.get_barrier_semaphore()
    pl.semaphore_signal(barrier, inc=1, device_id=partner, device_id_type=MESH_ID)

    @pl.when(core == 0)
    def _():
        for along in (along_x, along_z, along_y):
            for by in (1, 3):
                pl.semaphore_signal(barrier, inc=1, device_id=along(by), device_id_type=MESH_ID)
        pl.semaphore_wait(barrier, 7)

    @pl.when(core == 1)
    def _():
        pl.semaphore_wait(barrier, 1)

    def to_first():
        return pltpu.make_async_remote_copy(
            src_ref=total_ref, dst_ref=pair, send_sem=pair_sem.at[0], recv_sem=pair_sem.at[1],
            device_id=partner, device_id_type=MESH_ID)

    def to_second():
        return pltpu.make_async_remote_copy(
            src_ref=state, dst_ref=state, send_sem=state_sem.at[0], recv_sem=state_sem.at[1],
            device_id=partner, device_id_type=MESH_ID)

    def copy(level, hold, place, rows, k, target):
        return pltpu.make_async_remote_copy(
            src_ref=hold.at[place, rows], dst_ref=hold.at[place, rows],
            send_sem=send_sem.at[level, k], recv_sem=recv_sem.at[level, k],
            device_id=target, device_id_type=MESH_ID)

    def start(level, hold, p, along):
        right, left = along(1), along(3)
        copy(level, hold, p, upper, 0, right).start()
        copy(level, hold, p, lower, 2, left).start()
        copy(level, hold, p, lower, 1, right).start()
        copy(level, hold, p, upper, 3, left).start()

    def finish(level, hold, p, along):
        right, left = along(1), along(3)
        before, after, across = step(p, 3), step(p, 1), step(p, 2)
        copy(level, hold, before, upper, 0, right).wait_recv()
        copy(level, hold, before, upper, 4, right).start()
        copy(level, hold, after, lower, 2, left).wait_recv()
        copy(level, hold, after, lower, 5, left).start()
        copy(level, hold, before, lower, 1, right).wait_recv()
        copy(level, hold, after, upper, 3, left).wait_recv()
        copy(level, hold, across, upper, 4, right).wait_recv()
        copy(level, hold, across, lower, 5, left).wait_recv()

    def drain(level, hold, p, along):
        right, left = along(1), along(3)
        copy(level, hold, p, upper, 0, right).wait_send()
        copy(level, hold, p, lower, 1, right).wait_send()
        copy(level, hold, p, lower, 2, left).wait_send()
        copy(level, hold, p, upper, 3, left).wait_send()
        copy(level, hold, step(p, 3), upper, 4, right).wait_send()
        copy(level, hold, step(p, 1), lower, 5, left).wait_send()

    def reduce(hold):
        first = join(hold[0], hold[1], s)
        last = join(hold[2], hold[3], s)
        return first, join(first, last, s)

    def prefixes(hold, before, first):
        unit = jnp.where(eye(s), 1.0, 0.0).astype(f32)
        before[0] = jnp.concatenate([unit, jnp.zeros((s + PAD, s), f32)], axis=0)
        before[1] = hold[0]
        before[2] = first
        before[3] = join(first, hold[2], s)

    @pl.when(core == 1)
    def _():
        to_first().start()
        to_first().wait_send()
        to_second().wait_recv()
        entry_ref[...] = state[...]

    @pl.when(core == 0)
    def _():
        to_first().wait_recv()
        all_x[x] = join(total_ref[...], pair[...], s)
        start(0, all_x, x, along_x)
        finish(0, all_x, x, along_x)
        first, whole = reduce(all_x)
        all_z[z] = whole
        start(1, all_z, z, along_z)
        prefixes(all_x, before_x, first)
        finish(1, all_z, z, along_z)
        first, whole = reduce(all_z)
        all_y[y] = whole
        start(2, all_y, y, along_y)
        prefixes(all_z, before_z, first)
        here = join(before_z[z], before_x[x], s)
        chain[0] = here
        chain[1] = join(here, total_ref[...], s)
        finish(2, all_y, y, along_y)
        state[...] = jnp.concatenate(
            [jnp.where(eye(s), var_ref[...], 0.0), jnp.broadcast_to(mean_ref[...], (PAD, s))], axis=0)

        @pl.loop(0, y)
        def _(q):
            state[...] = join(state[...], all_y[q], 0)

        own = state[...]
        state[...] = join(own, chain[1], 0)
        to_second().start()
        entry_ref[...] = join(own, chain[0], 0)
        drain(0, all_x, x, along_x)
        drain(1, all_z, z, along_z)
        drain(2, all_y, y, along_y)
        to_second().wait_send()


def entry_of(total, init_mean, init_var):
    rows, s = total.shape
    vmem = pl.BlockSpec(memory_space=pltpu.VMEM)
    return pl.pallas_call(
        scan_kernel,
        in_specs=[vmem] * 3,
        out_specs=vmem,
        out_shape=jax.ShapeDtypeStruct((s + PAD, s), f32),
        scratch_shapes=[pltpu.VMEM((4, rows, s), f32)] * 5 + [
            pltpu.VMEM((2, rows, s), f32),
            pltpu.VMEM((rows, s), f32),
            pltpu.VMEM((s + PAD, s), f32),
            pltpu.SemaphoreType.DMA((3, 6)),
            pltpu.SemaphoreType.DMA((3, 6)),
            pltpu.SemaphoreType.DMA((2,)),
            pltpu.SemaphoreType.DMA((2,)),
        ],
        compiler_params=pltpu.CompilerParams(collective_id=0, has_side_effects=True),
        name="scan_devices",
    )(total, init_mean[None, :], init_var[None, :])


def per_device(
    init_mean, init_var, decay, coupling, obs_map, gain, noise_factor, obs_var, observed
):
    hi, lo, diag, shift, total = local_prefix(
        decay, coupling, obs_map, gain, noise_factor, obs_var, observed
    )
    entry = entry_of(total, init_mean, init_var)
    means, variances = outputs(entry, hi, lo, diag, shift)
    return (means, variances)


def solution(mesh):
    return jax.shard_map(
        per_device,
        mesh=mesh,
        in_specs=(
            P(),
            P(),
            P(("row", "col"), None),
            P(("row", "col"), None, None),
            P(("row", "col"), None, None),
            P(("row", "col"), None, None),
            P(),
            P(),
            P(("row", "col"), None),
        ),
        out_specs=(P(("row", "col"), None), P(("row", "col"), None)),
        check_vma=False,
    )
```

```python
import functools

import jax
import jax.numpy as jnp
from jax import lax
from jax.experimental import pallas as pl
from jax.experimental.pallas import tpu as pltpu
from jax.sharding import PartitionSpec as P

f32 = jnp.float32
bf16 = jnp.bfloat16
PAD = 16
SPB = 8


def dot_nn(a, b):
    return lax.dot_general(a, b, (((1,), (0,)), ((), ())), preferred_element_type=f32)


def dot_nt(a, b):
    return lax.dot_general(a, b, (((1,), (1,)), ((), ())), preferred_element_type=f32)


def split(x):
    hi = x.astype(bf16)
    return hi, (x - hi.astype(f32)).astype(bf16)


def eye(n):
    row = lax.broadcasted_iota(jnp.int32, (n, n), 0)
    col = lax.broadcasted_iota(jnp.int32, (n, n), 1)
    return row == col


def local_kernel(steps, decay_ref, observed_ref, var_ref, coupling_ref, map_ref, gain_ref,
                 factor_ref, hi_ref, lo_ref, diag_ref, shift_ref, total_ref, state, obs_var):
    i = pl.program_id(0)
    s = decay_ref.shape[1]

    @pl.when(i == 0)
    def _():
        unit = jnp.where(eye(s), 1.0, 0.0).astype(f32)
        state[...] = jnp.concatenate([unit, jnp.zeros((s + PAD, s), f32)], axis=0)
        obs_var[...] = jnp.broadcast_to(var_ref[...], obs_var.shape[::-1]).T

    factor = factor_ref[...]
    diagonal = eye(s)

    obs_gs = dot_nn(map_ref[...].reshape(-1, s), factor).astype(bf16)

    def build(j):
        t = i * steps + j
        decay = decay_ref[pl.ds(t, 1), :]
        obs_map = map_ref[j]
        gain = gain_ref[j]
        coupling = coupling_ref[j]
        gain_t = gain.T
        obs_f = (obs_map.astype(f32) * decay + dot_nn(obs_map, coupling)).astype(bf16)
        obs_g = obs_gs[j * obs_map.shape[0]:(j + 1) * obs_map.shape[0]]
        e = coupling.astype(f32) - dot_nn(gain_t, obs_f)
        e_hi, e_lo = split(e)
        shaped = (factor.astype(f32) - dot_nn(gain_t, obs_g)).astype(bf16)
        weighted = (gain.astype(f32) * obs_var[:, 0:1]).astype(bf16)
        noise = dot_nt(shaped, shaped) + dot_nn(gain_t, weighted)
        z_hi, z_lo = split(jnp.broadcast_to(observed_ref[pl.ds(t, 1), :], (PAD, gain.shape[0])))
        both = dot_nn(jnp.concatenate([z_hi, z_lo], axis=0), gain)
        shift = both[:PAD] + both[PAD:]
        decay_t = jnp.broadcast_to(decay, (8, s)).T[:, 0:1]
        return t, decay, decay_t, e_hi, e_lo, noise, shift

    maps = jnp.concatenate([state[:s], state[2 * s:]], axis=0)
    n = state[s:2 * s]
    ready = build(0)
    for j in range(steps):
        t, decay, decay_t, e_hi, e_lo, noise, shift = ready
        m_hi, m_lo = split(maps)
        moved = dot_nt(jnp.concatenate([n.astype(bf16), m_hi, m_lo], axis=0), e_hi)
        v = n * decay + moved[:s]
        y = maps * decay + (moved[s:2 * s + PAD] + (moved[2 * s + PAD:] + dot_nt(m_hi, e_lo)))
        b = y[s:] + shift
        maps = jnp.concatenate([y[:s], b], axis=0)
        o_hi, o_lo = split(y[:s])
        hi_ref[j] = o_hi
        lo_ref[j] = o_lo
        shift_ref[pl.ds(t, 1), :] = b[0:1]
        if j + 1 < steps:
            ready = build(j + 1)
        n = v * decay_t + noise + dot_nn(e_hi, v.astype(bf16))
        diag_ref[pl.ds(t, 1), :] = jnp.sum(jnp.where(diagonal, n, 0.0), axis=0, keepdims=True)
    state[:s] = maps[:s]
    state[s:2 * s] = n
    state[2 * s:] = maps[s:]

    @pl.when(i == pl.num_programs(0) - 1)
    def _():
        total_ref[...] = state[...]


def local_prefix(decay, coupling, obs_map, gain, factor, obs_var, observed):
    count, s = decay.shape
    m = obs_map.shape[1]
    steps = SPB
    block = lambda i: (i, 0, 0)
    whole = lambda i: (0, 0)
    return pl.pallas_call(
        functools.partial(local_kernel, steps),
        grid=(count // steps,),
        in_specs=[
            pl.BlockSpec((count, s), whole),
            pl.BlockSpec((count, m), whole),
            pl.BlockSpec((1, m), whole),
            pl.BlockSpec((steps, s, s), block),
            pl.BlockSpec((steps, m, s), block),
            pl.BlockSpec((steps, m, s), block),
            pl.BlockSpec((s, s), whole),
        ],
        out_specs=[
            pl.BlockSpec((steps, s, s), block),
            pl.BlockSpec((steps, s, s), block),
            pl.BlockSpec((count, s), whole),
            pl.BlockSpec((count, s), whole),
            pl.BlockSpec((2 * s + PAD, s), whole),
        ],
        out_shape=[
            jax.ShapeDtypeStruct((count, s, s), bf16),
            jax.ShapeDtypeStruct((count, s, s), bf16),
            jax.ShapeDtypeStruct((count, s), f32),
            jax.ShapeDtypeStruct((count, s), f32),
            jax.ShapeDtypeStruct((2 * s + PAD, s), f32),
        ],
        scratch_shapes=[
            pltpu.VMEM((2 * s + PAD, s), f32),
            pltpu.VMEM((m, 8), f32),
        ],
        name="local_prefix",
    )(decay, observed, obs_var[None, :], coupling, obs_map, gain, factor)


def output_kernel(steps, entry_ref, hi_ref, lo_ref, diag_ref, shift_ref, mean_ref, var_ref, left):
    i = pl.program_id(0)
    s = hi_ref.shape[2]
    rows = s + PAD

    @pl.when(i == 0)
    def _():
        hi, lo = split(entry_ref[...])
        left[:rows] = hi
        left[rows:] = lo

    for j in range(steps):
        t = i * steps + j
        hi, lo = hi_ref[j], lo_ref[j]
        both = dot_nn(left[...], hi)
        r = both[:rows] + (both[rows:] + dot_nn(left[:rows], lo))
        maps = hi.astype(f32) + lo.astype(f32)
        var_ref[pl.ds(t, 1), :] = (
            jnp.sum(r[:s] * maps, axis=0, keepdims=True) + diag_ref[pl.ds(t, 1), :]
        )
        mean_ref[pl.ds(t, 1), :] = r[s:s + 1] + shift_ref[pl.ds(t, 1), :]


def outputs(entry, hi, lo, diag, shift):
    count, s = diag.shape
    steps = SPB
    whole = lambda i: (0, 0)
    return pl.pallas_call(
        functools.partial(output_kernel, steps),
        grid=(count // steps,),
        in_specs=[
            pl.BlockSpec((s + PAD, s), whole),
            pl.BlockSpec((steps, s, s), lambda i: (i, 0, 0)),
            pl.BlockSpec((steps, s, s), lambda i: (i, 0, 0)),
            pl.BlockSpec((count, s), whole),
            pl.BlockSpec((count, s), whole),
        ],
        out_specs=[pl.BlockSpec((count, s), whole), pl.BlockSpec((count, s), whole)],
        out_shape=[jax.ShapeDtypeStruct((count, s), f32)] * 2,
        scratch_shapes=[pltpu.VMEM((2 * (s + PAD), s), bf16)],
        name="outputs",
    )(entry, hi, lo, diag, shift)


MESH_ID = pl.DeviceIdType.MESH


def join(first, later, lead):
    s = later.shape[1]
    t_hi, t_lo = split(later[:s])
    x_hi, x_lo = split(first)
    y = dot_nn(x_hi, t_hi) + (dot_nn(x_lo, t_hi) + dot_nn(x_hi, t_lo))
    v_hi, v_lo = split(y[lead:lead + s])
    u_hi, u_lo = t_hi.T, t_lo.T
    n = dot_nn(u_hi, v_hi) + (dot_nn(u_hi, v_lo) + dot_nn(u_lo, v_hi)) + later[s:2 * s]
    b = y[lead + s:] + later[2 * s:]
    parts = [y[:lead], n, b] if lead else [n, b]
    return jnp.concatenate(parts, axis=0)


def scan_kernel(total_ref, mean_ref, var_ref, entry_ref, all_x, all_z, all_y, before_x, before_z,
                chain, pair, state, send_sem, recv_sem, pair_sem, state_sem):
    row, col = lax.axis_index("row"), lax.axis_index("col")
    y, z = row // 4, lax.rem(row, 4)
    x, core = col // 2, lax.rem(col, 2)
    s = total_ref.shape[1]
    half = total_ref.shape[0] // 2
    upper, lower = pl.ds(0, half), pl.ds(half, half)

    def step(p, by):
        return lax.rem(p + by, 4)

    def along_x(by):
        return (row, step(x, by) * 2 + core)

    def along_z(by):
        return (y * 4 + step(z, by), col)

    def along_y(by):
        return (step(y, by) * 4 + z, col)

    partner = (row, x * 2 + 1 - core)
    barrier = pltpu.get_barrier_semaphore()
    pl.semaphore_signal(barrier, inc=1, device_id=partner, device_id_type=MESH_ID)

    @pl.when(core == 0)
    def _():
        for along in (along_x, along_z, along_y):
            for by in (1, 3):
                pl.semaphore_signal(barrier, inc=1, device_id=along(by), device_id_type=MESH_ID)
        pl.semaphore_wait(barrier, 7)

    @pl.when(core == 1)
    def _():
        pl.semaphore_wait(barrier, 1)

    def to_first():
        return pltpu.make_async_remote_copy(
            src_ref=total_ref, dst_ref=pair, send_sem=pair_sem.at[0], recv_sem=pair_sem.at[1],
            device_id=partner, device_id_type=MESH_ID)

    def to_second():
        return pltpu.make_async_remote_copy(
            src_ref=state, dst_ref=state, send_sem=state_sem.at[0], recv_sem=state_sem.at[1],
            device_id=partner, device_id_type=MESH_ID)

    def copy(level, hold, place, rows, k, target):
        return pltpu.make_async_remote_copy(
            src_ref=hold.at[place, rows], dst_ref=hold.at[place, rows],
            send_sem=send_sem.at[level, k], recv_sem=recv_sem.at[level, k],
            device_id=target, device_id_type=MESH_ID)

    def start(level, hold, p, along):
        right, left = along(1), along(3)
        copy(level, hold, p, upper, 0, right).start()
        copy(level, hold, p, lower, 2, left).start()
        copy(level, hold, p, lower, 1, right).start()
        copy(level, hold, p, upper, 3, left).start()

    def finish(level, hold, p, along):
        right, left = along(1), along(3)
        before, after, across = step(p, 3), step(p, 1), step(p, 2)
        copy(level, hold, before, upper, 0, right).wait_recv()
        copy(level, hold, before, upper, 4, right).start()
        copy(level, hold, after, lower, 2, left).wait_recv()
        copy(level, hold, after, lower, 5, left).start()
        copy(level, hold, before, lower, 1, right).wait_recv()
        copy(level, hold, after, upper, 3, left).wait_recv()
        copy(level, hold, across, upper, 4, right).wait_recv()
        copy(level, hold, across, lower, 5, left).wait_recv()

    def drain(level, hold, p, along):
        right, left = along(1), along(3)
        copy(level, hold, p, upper, 0, right).wait_send()
        copy(level, hold, p, lower, 1, right).wait_send()
        copy(level, hold, p, lower, 2, left).wait_send()
        copy(level, hold, p, upper, 3, left).wait_send()
        copy(level, hold, step(p, 3), upper, 4, right).wait_send()
        copy(level, hold, step(p, 1), lower, 5, left).wait_send()

    def reduce(hold):
        first = join(hold[0], hold[1], s)
        last = join(hold[2], hold[3], s)
        return first, join(first, last, s)

    def prefixes(hold, before, first):
        unit = jnp.where(eye(s), 1.0, 0.0).astype(f32)
        before[0] = jnp.concatenate([unit, jnp.zeros((s + PAD, s), f32)], axis=0)
        before[1] = hold[0]
        before[2] = first
        before[3] = join(first, hold[2], s)

    @pl.when(core == 1)
    def _():
        to_first().start()
        to_first().wait_send()
        to_second().wait_recv()
        entry_ref[...] = state[...]

    @pl.when(core == 0)
    def _():
        to_first().wait_recv()
        all_x[x] = join(total_ref[...], pair[...], s)
        start(0, all_x, x, along_x)
        finish(0, all_x, x, along_x)
        first, whole = reduce(all_x)
        all_z[z] = whole
        start(1, all_z, z, along_z)
        prefixes(all_x, before_x, first)
        finish(1, all_z, z, along_z)
        first, whole = reduce(all_z)
        all_y[y] = whole
        start(2, all_y, y, along_y)
        prefixes(all_z, before_z, first)
        here = join(before_z[z], before_x[x], s)
        chain[0] = here
        chain[1] = join(here, total_ref[...], s)
        finish(2, all_y, y, along_y)
        state[...] = jnp.concatenate(
            [jnp.where(eye(s), var_ref[...], 0.0), jnp.broadcast_to(mean_ref[...], (PAD, s))], axis=0)

        @pl.loop(0, y)
        def _(q):
            state[...] = join(state[...], all_y[q], 0)

        own = state[...]
        state[...] = join(own, chain[1], 0)
        to_second().start()
        entry_ref[...] = join(own, chain[0], 0)
        drain(0, all_x, x, along_x)
        drain(1, all_z, z, along_z)
        drain(2, all_y, y, along_y)
        to_second().wait_send()


def entry_of(total, init_mean, init_var):
    rows, s = total.shape
    vmem = pl.BlockSpec(memory_space=pltpu.VMEM)
    return pl.pallas_call(
        scan_kernel,
        in_specs=[vmem] * 3,
        out_specs=vmem,
        out_shape=jax.ShapeDtypeStruct((s + PAD, s), f32),
        scratch_shapes=[pltpu.VMEM((4, rows, s), f32)] * 5 + [
            pltpu.VMEM((2, rows, s), f32),
            pltpu.VMEM((rows, s), f32),
            pltpu.VMEM((s + PAD, s), f32),
            pltpu.SemaphoreType.DMA((3, 6)),
            pltpu.SemaphoreType.DMA((3, 6)),
            pltpu.SemaphoreType.DMA((2,)),
            pltpu.SemaphoreType.DMA((2,)),
        ],
        compiler_params=pltpu.CompilerParams(collective_id=0, has_side_effects=True),
        name="scan_devices",
    )(total, init_mean[None, :], init_var[None, :])


def per_device(
    init_mean, init_var, decay, coupling, obs_map, gain, noise_factor, obs_var, observed
):
    hi, lo, diag, shift, total = local_prefix(
        decay, coupling, obs_map, gain, noise_factor, obs_var, observed
    )
    entry = entry_of(total, init_mean, init_var)
    means, variances = outputs(entry, hi, lo, diag, shift)
    return (means, variances)


def solution(mesh):
    return jax.shard_map(
        per_device,
        mesh=mesh,
        in_specs=(
            P(),
            P(),
            P(("row", "col"), None),
            P(("row", "col"), None, None),
            P(("row", "col"), None, None),
            P(("row", "col"), None, None),
            P(),
            P(),
            P(("row", "col"), None),
        ),
        out_specs=(P(("row", "col"), None), P(("row", "col"), None)),
        check_vma=False,
    )
```

```python
import functools

import jax
import jax.numpy as jnp
from jax import lax
from jax.experimental import pallas as pl
from jax.experimental.pallas import tpu as pltpu
from jax.sharding import PartitionSpec as P

f32 = jnp.float32
bf16 = jnp.bfloat16
PAD = 16
SPB = 4


def dot_nn(a, b):
    return lax.dot_general(a, b, (((1,), (0,)), ((), ())), preferred_element_type=f32)


def dot_nt(a, b):
    return lax.dot_general(a, b, (((1,), (1,)), ((), ())), preferred_element_type=f32)


def split(x):
    hi = x.astype(bf16)
    return hi, (x - hi.astype(f32)).astype(bf16)


def eye(n):
    row = lax.broadcasted_iota(jnp.int32, (n, n), 0)
    col = lax.broadcasted_iota(jnp.int32, (n, n), 1)
    return row == col


MESH_ID = pl.DeviceIdType.MESH


def product(a, b):
    a_hi, a_lo = split(a)
    b_hi, b_lo = split(b)
    return dot_nn(a_hi, b_hi) + (dot_nn(a_lo, b_hi) + dot_nn(a_hi, b_lo))


def moved(part, maps):
    s = maps.shape[0]
    t_hi, t_lo = split(maps)
    x_hi, x_lo = split(part)
    y = dot_nn(x_hi, t_hi) + (dot_nn(x_lo, t_hi) + dot_nn(x_hi, t_lo))
    v_hi, v_lo = split(y[:s])
    u_hi, u_lo = t_hi.T, t_lo.T
    n = dot_nn(u_hi, v_hi) + (dot_nn(u_hi, v_lo) + dot_nn(u_lo, v_hi))
    return jnp.concatenate([n, y[s:]], axis=0)


def pack(part):
    s = part.shape[1]
    h, k = s // 2, s // 4
    square = jnp.concatenate([part[h:h + k, h:], part[h + k:s, h:]], axis=1)
    return jnp.concatenate([part[:h], square, part[s:s + 8]], axis=0)


def unpack(packed):
    s = packed.shape[1]
    h, k = s // 2, s // 4
    top, square, shift = packed[:h], packed[h:h + k], packed[h + k:]
    corner = jnp.concatenate([square[:, :h], square[:, h:]], axis=0)
    low = jnp.concatenate([top[:, h:].T, corner], axis=1)
    return jnp.concatenate([top, low] + [shift] * (PAD // 8), axis=0)


def maps_kernel(steps, decay_ref, observed_ref, coupling_ref, map_ref, gain_ref,
                step_ref, maps_ref, shift_ref, total_ref, state):
    i = pl.program_id(0)
    s = decay_ref.shape[1]
    half = decay_ref.shape[0] // 2

    @pl.when(i == 0)
    def _():
        unit = jnp.where(eye(s), 1.0, 0.0).astype(f32)
        for h in range(2):
            state[h] = jnp.concatenate([unit, jnp.zeros((PAD, s), f32)], axis=0)

    def build(h, j):
        t = h * half + i * steps + j
        decay = decay_ref[pl.ds(t, 1), :]
        obs_map, gain, coupling = map_ref[h, j], gain_ref[h, j], coupling_ref[h, j]
        obs_f = (obs_map.astype(f32) * decay + dot_nn(obs_map, coupling)).astype(bf16)
        e_hi, e_lo = split(coupling.astype(f32) - dot_nn(gain.T, obs_f))
        step_ref[h, j] = e_hi
        z_hi, z_lo = split(jnp.broadcast_to(observed_ref[pl.ds(t, 1), :], (PAD, gain.shape[0])))
        both = dot_nn(jnp.concatenate([z_hi, z_lo], axis=0), gain)
        return t, decay, e_hi, e_lo, both[:PAD] + both[PAD:]

    maps = [state[0], state[1]]
    ready = [build(0, 0), build(1, 0)]
    for j in range(steps):
        for h in range(2):
            t, decay, e_hi, e_lo, shift = ready[h]
            m_hi, m_lo = split(maps[h])
            moved = dot_nt(jnp.concatenate([m_hi, m_lo], axis=0), e_hi)
            y = maps[h] * decay + (moved[:s + PAD] + (moved[s + PAD:] + dot_nt(m_hi, e_lo)))
            b = y[s:] + shift
            maps_ref[h, j] = y[:s]
            shift_ref[pl.ds(t, 1), :] = b[0:1]
            maps[h] = jnp.concatenate([y[:s], b], axis=0)
            if j + 1 < steps:
                ready[h] = build(h, j + 1)
    for h in range(2):
        state[h] = maps[h]

    @pl.when(i == pl.num_programs(0) - 1)
    def _():
        total_ref[...] = state[...]


def halves(a):
    return a.reshape((2, a.shape[0] // 2) + a.shape[1:])


def whole(i):
    return (0, 0)


def local_maps(decay, coupling, obs_map, gain, observed):
    count, s = decay.shape
    m = obs_map.shape[1]
    steps = SPB
    block = lambda i: (0, i, 0, 0)
    square = pl.BlockSpec((2, steps, s, s), block)
    flat = pl.BlockSpec((2, steps, m, s), block)
    return pl.pallas_call(
        functools.partial(maps_kernel, steps),
        grid=(count // (2 * steps),),
        in_specs=[pl.BlockSpec((count, s), whole), pl.BlockSpec((count, m), whole),
                  square, flat, flat],
        out_specs=[square, square, pl.BlockSpec((count, s), whole),
                   pl.BlockSpec((2, s + PAD, s), lambda i: (0, 0, 0))],
        out_shape=[
            jax.ShapeDtypeStruct((2, count // 2, s, s), bf16),
            jax.ShapeDtypeStruct((2, count // 2, s, s), f32),
            jax.ShapeDtypeStruct((count, s), f32),
            jax.ShapeDtypeStruct((2, s + PAD, s), f32),
        ],
        scratch_shapes=[pltpu.VMEM((2, s + PAD, s), f32)],
        name="local_maps",
    )(decay, observed, halves(coupling), halves(obs_map), halves(gain))


def scan_kernel(steps, decay_ref, var_ref, factor_ref, map_ref, gain_ref, step_ref, total_ref,
                mean0_ref, var0_ref, entry_ref, diag_ref,
                noise, obs_var, own_map, own_part, map_x, map_z, map_y, part_x, part_z, part_y,
                later, before, pair_map, pair_part, state,
                send_sem, recv_sem, pair_sem):
    i = pl.program_id(0)
    last = pl.num_programs(0) - 1
    row, col = lax.axis_index("row"), lax.axis_index("col")
    y, z = row // 4, lax.rem(row, 4)
    x, core = col // 2, lax.rem(col, 2)
    s = decay_ref.shape[1]
    half = decay_ref.shape[0] // 2

    def step(p, by):
        return lax.rem(p + by, 4)

    def along_x(by):
        return (row, step(x, by) * 2 + core)

    def along_z(by):
        return (y * 4 + step(z, by), col)

    def along_y(by):
        return (step(y, by) * 4 + z, col)

    partner = (row, x * 2 + 1 - core)

    def on_chip(source, target, k):
        return pltpu.make_async_remote_copy(
            src_ref=source, dst_ref=target, send_sem=pair_sem.at[0, k],
            recv_sem=pair_sem.at[1, k], device_id=partner, device_id_type=MESH_ID)

    def copy(level, kind, hold, p, along, by, source=0):
        slot = step(p, source)
        return pltpu.make_async_remote_copy(
            src_ref=hold.at[slot], dst_ref=hold.at[slot],
            send_sem=send_sem.at[level, kind, by - 1], recv_sem=recv_sem.at[level, kind, by - 1],
            device_id=along(by), device_id_type=MESH_ID)

    class Ring:
        def __init__(self, *what):
            self.what = what
            self.hold, self.p = what[2], what[3]

        def start(self):
            for by in (1, 3, 2):
                copy(*self.what, by).start()

        def arrived(self, by):
            copy(*self.what, by, source=4 - by).wait_recv()
            return step(self.p, 4 - by)

        def drain(self):
            for by in (1, 3, 2):
                copy(*self.what, by).wait_send()

    mx, px = Ring(0, 0, map_x, x, along_x), Ring(0, 1, part_x, x, along_x)
    mz, pz = Ring(1, 0, map_z, z, along_z), Ring(1, 1, part_z, z, along_z)
    my, py = Ring(2, 0, map_y, y, along_y), Ring(2, 1, part_y, y, along_y)

    @pl.when(i == 0)
    def _():
        barrier = pltpu.get_barrier_semaphore()
        pl.semaphore_signal(barrier, inc=1, device_id=partner, device_id_type=MESH_ID)
        for along in (along_x, along_z, along_y):
            for by in (1, 2, 3):
                pl.semaphore_signal(barrier, inc=1, device_id=along(by), device_id_type=MESH_ID)
        noise[...] = jnp.zeros_like(noise)
        obs_var[...] = jnp.broadcast_to(var_ref[...], obs_var.shape[::-1]).T
        own_map[...] = product(total_ref[0, :s], total_ref[1, :s])
        pl.semaphore_wait(barrier, 10)

        @pl.when(core == 1)
        def _():
            on_chip(own_map, pair_map, 0).start()

    @pl.when(jnp.logical_and(i == 0, core == 0))
    def _():
        on_chip(own_map, pair_map, 0).wait_recv()
        map_x[x] = product(own_map[...], pair_map[...])
        mx.start()

    factor = factor_ref[...]
    diagonal = eye(s)
    m = map_ref.shape[2]
    obs_gs = dot_nn(map_ref[...].reshape(-1, s), factor).astype(bf16)

    def build(h, j):
        t = h * half + i * steps + j
        gain = gain_ref[h, j]
        gain_t = gain.T
        k = h * steps + j
        shaped = (factor.astype(f32) - dot_nn(gain_t, obs_gs[k * m:(k + 1) * m])).astype(bf16)
        weighted = (gain.astype(f32) * obs_var[:, 0:1]).astype(bf16)
        decay = decay_ref[pl.ds(t, 1), :]
        decay_t = jnp.broadcast_to(decay, (8, s)).T[:, 0:1]
        return t, decay, decay_t, dot_nt(shaped, shaped) + dot_nn(gain_t, weighted)

    ns = [noise[0], noise[1]]
    ready = [build(0, 0), build(1, 0)]
    for j in range(steps):
        for h in range(2):
            t, decay, decay_t, fresh = ready[h]
            e = step_ref[h, j]
            v = ns[h] * decay + dot_nt(ns[h].astype(bf16), e)
            if j + 1 < steps:
                ready[h] = build(h, j + 1)
            n = v * decay_t + fresh + dot_nn(e, v.astype(bf16))
            diag_ref[pl.ds(t, 1), :] = jnp.sum(jnp.where(diagonal, n, 0.0), axis=0, keepdims=True)
            ns[h] = n
    for h in range(2):
        noise[h] = ns[h]

    def pairs(maps):
        m01 = product(maps[0], maps[1])
        m23 = product(maps[2], maps[3])
        return m01, m23

    def suffixes(maps, m23):
        later[3] = jnp.where(eye(s), 1.0, 0.0).astype(f32)
        later[2] = maps[3]
        later[1] = m23
        later[0] = product(maps[1], m23)

    def earlier_map(p, maps, m01):
        m012 = product(m01, maps[2])
        unit = jnp.where(eye(s), 1.0, 0.0).astype(f32)
        low = jnp.where(p == 0, unit, maps[0])
        return jnp.where(p < 2, low, jnp.where(p == 2, m01, m012))

    def earlier_part(p, parts, maps):
        p0 = unpack(parts[0])
        p01 = moved(p0, maps[1]) + unpack(parts[1])
        p012 = moved(p01, maps[2]) + unpack(parts[2])
        low = jnp.where(p == 0, 0.0, p0)
        return jnp.where(p < 2, low, jnp.where(p == 2, p01, p012))

    def total_part(ring, p):
        parts = ring.hold
        sum_ = moved(unpack(parts[p]), later[p])
        left, right = ring.arrived(1), ring.arrived(3)
        sum_ = sum_ + moved(unpack(parts[left]), later[left])
        sum_ = sum_ + moved(unpack(parts[right]), later[right])
        across = ring.arrived(2)
        return pack(sum_ + moved(unpack(parts[across]), later[across]))

    def first_half():
        return jnp.concatenate([noise[0], total_ref[0, s:]], axis=0)

    @pl.when(i == last)
    def _():
        second = jnp.concatenate([noise[1], total_ref[1, s:]], axis=0)
        own_part[...] = moved(first_half(), total_ref[1, :s]) + second

    @pl.when(jnp.logical_and(i == last, core == 1))
    def _():
        on_chip(own_part, pair_part, 1).start()
        on_chip(own_map, pair_map, 0).wait_send()
        on_chip(own_part, pair_part, 1).wait_send()
        on_chip(state, state, 2).wait_recv()
        entry = unpack(state[...])
        entry_ref[0] = entry
        entry_ref[1] = moved(entry, total_ref[0, :s]) + first_half()

    @pl.when(jnp.logical_and(i == last, core == 0))
    def _():
        for by in (1, 3, 2):
            mx.arrived(by)
        x01, x23 = pairs(map_x)
        map_z[z] = product(x01, x23)
        mz.start()
        on_chip(own_part, pair_part, 1).wait_recv()
        part_x[x] = pack(moved(own_part[...], pair_map[...]) + pair_part[...])
        px.start()
        suffixes(map_x, x23)
        before[0] = earlier_map(x, map_x, x01)
        part_z[z] = total_part(px, x)
        pz.start()
        for by in (1, 3, 2):
            mz.arrived(by)
        z01, z23 = pairs(map_z)
        map_y[y] = product(z01, z23)
        my.start()
        suffixes(map_z, z23)
        near = earlier_part(x, part_x, map_x)
        before[3] = product(earlier_map(z, map_z, z01), before[0])
        part_y[y] = total_part(pz, z)
        py.start()
        near = near + moved(earlier_part(z, part_z, map_z), before[0])
        for by in (1, 3, 2):
            my.arrived(by)
        for q in (2, 1, 0):
            after = before[q + 1]
            before[q] = jnp.where(q < y, product(map_y[q], after), after)
        t0 = before[0]
        weights = jnp.broadcast_to(var0_ref[...], (8, s)).T[:, 0:1]
        u_hi, u_lo = split(t0)
        w_hi, w_lo = split(t0 * weights)
        u_hi_t, u_lo_t = u_hi.T, u_lo.T
        start_noise = dot_nn(u_hi_t, w_hi) + (dot_nn(u_hi_t, w_lo) + dot_nn(u_lo_t, w_hi))
        start_mean = product(jnp.broadcast_to(mean0_ref[...], (PAD, s)), t0)
        near = near + jnp.concatenate([start_noise, start_mean], axis=0)
        for by in (1, 3, 2):
            q = py.arrived(by)
            part = moved(unpack(part_y[q]), before[jnp.minimum(q + 1, 3)])
            near = near + jnp.where(q < y, part, 0.0)
        state[...] = pack(moved(near, own_map[...]) + own_part[...])
        on_chip(state, state, 2).start()
        entry_ref[0] = near
        entry_ref[1] = moved(near, total_ref[0, :s]) + first_half()
        for ring in (mx, px, mz, pz, my, py):
            ring.drain()
        on_chip(state, state, 2).wait_send()


def scan(decay, obs_var, factor, obs_map, gain, step_maps, total, init_mean, init_var):
    count, s = decay.shape
    m = obs_map.shape[1]
    steps = SPB
    rows = s + PAD
    packed = s // 2 + s // 4 + 8
    block = lambda i: (0, i, 0, 0)
    flat = pl.BlockSpec((2, steps, m, s), block)
    three = lambda i: (0, 0, 0)
    return pl.pallas_call(
        functools.partial(scan_kernel, steps),
        grid=(count // (2 * steps),),
        in_specs=[
            pl.BlockSpec((count, s), whole),
            pl.BlockSpec((1, m), whole),
            pl.BlockSpec((s, s), whole),
            flat,
            flat,
            pl.BlockSpec((2, steps, s, s), block),
            pl.BlockSpec((2, rows, s), three),
            pl.BlockSpec((1, s), whole),
            pl.BlockSpec((1, s), whole),
        ],
        out_specs=[pl.BlockSpec((2, rows, s), three), pl.BlockSpec((count, s), whole)],
        out_shape=[
            jax.ShapeDtypeStruct((2, rows, s), f32),
            jax.ShapeDtypeStruct((count, s), f32),
        ],
        scratch_shapes=[
            pltpu.VMEM((2, s, s), f32),
            pltpu.VMEM((m, 8), f32),
            pltpu.VMEM((s, s), f32),
            pltpu.VMEM((rows, s), f32),
        ] + [pltpu.VMEM((4, s, s), f32)] * 3 + [pltpu.VMEM((4, packed, s), f32)] * 3 + [
            pltpu.VMEM((4, s, s), f32),
            pltpu.VMEM((4, s, s), f32),
            pltpu.VMEM((s, s), f32),
            pltpu.VMEM((rows, s), f32),
            pltpu.VMEM((packed, s), f32),
            pltpu.SemaphoreType.DMA((3, 2, 3)),
            pltpu.SemaphoreType.DMA((3, 2, 3)),
            pltpu.SemaphoreType.DMA((2, 3)),
        ],
        compiler_params=pltpu.CompilerParams(collective_id=0, has_side_effects=True),
        name="scan_devices",
    )(decay, obs_var[None, :], factor, halves(obs_map), halves(gain), step_maps, total,
      init_mean[None, :], init_var[None, :])


def output_kernel(steps, entry_ref, maps_ref, diag_ref, shift_ref, mean_ref, var_ref,
                  off, straight, first_mean):
    i = pl.program_id(0)
    s = maps_ref.shape[3]
    half = diag_ref.shape[0] // 2

    @pl.when(i == 0)
    def _():
        diagonal = eye(s)
        for h in range(2):
            cov = entry_ref[h, :s]
            off[h] = jnp.where(diagonal, 0.0, cov).astype(bf16)
            held = jnp.sum(jnp.where(diagonal, cov, 0.0), axis=1, keepdims=True)
            straight[h] = jnp.broadcast_to(held, (s, s))
            first_mean[h] = jnp.broadcast_to(entry_ref[h, s:s + 8].T[:, 0:1], (s, s))

    for j in range(steps):
        for h in range(2):
            t = h * half + i * steps + j
            maps = maps_ref[h, j]
            r = dot_nn(off[h], maps.astype(bf16)) + straight[h] * maps
            var_ref[pl.ds(t, 1), :] = (
                jnp.sum(r * maps, axis=0, keepdims=True) + diag_ref[pl.ds(t, 1), :]
            )
            mean_ref[pl.ds(t, 1), :] = (
                jnp.sum(first_mean[h] * maps, axis=0, keepdims=True) + shift_ref[pl.ds(t, 1), :]
            )


def outputs(entry, maps, diag, shift):
    count, s = diag.shape
    steps = SPB
    full = pl.BlockSpec((count, s), whole)
    return pl.pallas_call(
        functools.partial(output_kernel, steps),
        grid=(count // (2 * steps),),
        in_specs=[
            pl.BlockSpec((2, s + PAD, s), lambda i: (0, 0, 0)),
            pl.BlockSpec((2, steps, s, s), lambda i: (0, i, 0, 0)),
            full,
            full,
        ],
        out_specs=[full, full],
        out_shape=[jax.ShapeDtypeStruct((count, s), f32)] * 2,
        scratch_shapes=[
            pltpu.VMEM((2, s, s), bf16),
            pltpu.VMEM((2, s, s), f32),
            pltpu.VMEM((2, s, s), f32),
        ],
        name="outputs",
    )(entry, maps, diag, shift)


def per_device(
    init_mean, init_var, decay, coupling, obs_map, gain, noise_factor, obs_var, observed
):
    step_maps, maps, shift, total = local_maps(decay, coupling, obs_map, gain, observed)
    entry, diag = scan(
        decay, obs_var, noise_factor, obs_map, gain, step_maps, total, init_mean, init_var
    )
    means, variances = outputs(entry, maps, diag, shift)
    return (means, variances)


def solution(mesh):
    return jax.shard_map(
        per_device,
        mesh=mesh,
        in_specs=(
            P(),
            P(),
            P(("row", "col"), None),
            P(("row", "col"), None, None),
            P(("row", "col"), None, None),
            P(("row", "col"), None, None),
            P(),
            P(),
            P(("row", "col"), None),
        ),
        out_specs=(P(("row", "col"), None), P(("row", "col"), None)),
        check_vma=False,
    )
```

```python
import functools

import jax
import jax.numpy as jnp
from jax import lax
from jax.experimental import pallas as pl
from jax.experimental.pallas import tpu as pltpu
from jax.sharding import PartitionSpec as P

f32 = jnp.float32
bf16 = jnp.bfloat16
PAD = 16
SPB = 4


def dot_nn(a, b):
    return lax.dot_general(a, b, (((1,), (0,)), ((), ())), preferred_element_type=f32)


def dot_nt(a, b):
    return lax.dot_general(a, b, (((1,), (1,)), ((), ())), preferred_element_type=f32)


def split(x):
    hi = x.astype(bf16)
    return hi, (x - hi.astype(f32)).astype(bf16)


def eye(n):
    row = lax.broadcasted_iota(jnp.int32, (n, n), 0)
    col = lax.broadcasted_iota(jnp.int32, (n, n), 1)
    return row == col


MESH_ID = pl.DeviceIdType.MESH


def product(a, b):
    a_hi, a_lo = split(a)
    b_hi, b_lo = split(b)
    return dot_nn(a_hi, b_hi) + (dot_nn(a_lo, b_hi) + dot_nn(a_hi, b_lo))


def moved(part, maps):
    s = maps.shape[0]
    t_hi, t_lo = split(maps)
    x_hi, x_lo = split(part)
    y = dot_nn(x_hi, t_hi) + (dot_nn(x_lo, t_hi) + dot_nn(x_hi, t_lo))
    v_hi, v_lo = split(y[:s])
    u_hi, u_lo = t_hi.T, t_lo.T
    n = dot_nn(u_hi, v_hi) + (dot_nn(u_hi, v_lo) + dot_nn(u_lo, v_hi))
    return jnp.concatenate([n, y[s:]], axis=0)


def pack(part):
    s = part.shape[1]
    h, k = s // 2, s // 4
    square = jnp.concatenate([part[h:h + k, h:], part[h + k:s, h:]], axis=1)
    return jnp.concatenate([part[:h], square, part[s:s + 8]], axis=0)


def unpack(packed):
    s = packed.shape[1]
    h, k = s // 2, s // 4
    top, square, shift = packed[:h], packed[h:h + k], packed[h + k:]
    corner = jnp.concatenate([square[:, :h], square[:, h:]], axis=0)
    low = jnp.concatenate([top[:, h:].T, corner], axis=1)
    return jnp.concatenate([top, low] + [shift] * (PAD // 8), axis=0)


def maps_kernel(steps, decay_ref, observed_ref, coupling_ref, map_ref, gain_ref,
                step_ref, maps_ref, shift_ref, total_ref, state):
    i = pl.program_id(0)
    s = decay_ref.shape[1]
    half = decay_ref.shape[0] // 2

    @pl.when(i == 0)
    def _():
        unit = jnp.where(eye(s), 1.0, 0.0).astype(f32)
        for h in range(2):
            state[h] = jnp.concatenate([unit, jnp.zeros((PAD, s), f32)], axis=0)

    def build(h, j):
        t = h * half + i * steps + j
        decay = decay_ref[pl.ds(t, 1), :]
        obs_map, gain, coupling = map_ref[h, j], gain_ref[h, j], coupling_ref[h, j]
        obs_f = (obs_map.astype(f32) * decay + dot_nn(obs_map, coupling)).astype(bf16)
        e_hi, e_lo = split(coupling.astype(f32) - dot_nn(gain.T, obs_f))
        step_ref[h, j] = e_hi
        z_hi, z_lo = split(jnp.broadcast_to(observed_ref[pl.ds(t, 1), :], (PAD, gain.shape[0])))
        both = dot_nn(jnp.concatenate([z_hi, z_lo], axis=0), gain)
        return t, decay, e_hi, e_lo, both[:PAD] + both[PAD:]

    maps = [state[0], state[1]]
    ready = [build(0, 0), build(1, 0)]
    for j in range(steps):
        for h in range(2):
            t, decay, e_hi, e_lo, shift = ready[h]
            m_hi, m_lo = split(maps[h])
            moved = dot_nt(jnp.concatenate([m_hi, m_lo], axis=0), e_hi)
            y = maps[h] * decay + (moved[:s + PAD] + (moved[s + PAD:] + dot_nt(m_hi, e_lo)))
            b = y[s:] + shift
            maps_ref[h, j] = y[:s]
            shift_ref[pl.ds(t, 1), :] = b[0:1]
            maps[h] = jnp.concatenate([y[:s], b], axis=0)
            if j + 1 < steps:
                ready[h] = build(h, j + 1)
    for h in range(2):
        state[h] = maps[h]

    @pl.when(i == pl.num_programs(0) - 1)
    def _():
        total_ref[...] = state[...]


def halves(a):
    return a.reshape((2, a.shape[0] // 2) + a.shape[1:])


def whole(i):
    return (0, 0)


def local_maps(decay, coupling, obs_map, gain, observed):
    count, s = decay.shape
    m = obs_map.shape[1]
    steps = SPB
    block = lambda i: (0, i, 0, 0)
    square = pl.BlockSpec((2, steps, s, s), block)
    flat = pl.BlockSpec((2, steps, m, s), block)
    return pl.pallas_call(
        functools.partial(maps_kernel, steps),
        grid=(count // (2 * steps),),
        in_specs=[pl.BlockSpec((count, s), whole), pl.BlockSpec((count, m), whole),
                  square, flat, flat],
        out_specs=[square, square, pl.BlockSpec((count, s), whole),
                   pl.BlockSpec((2, s + PAD, s), lambda i: (0, 0, 0))],
        out_shape=[
            jax.ShapeDtypeStruct((2, count // 2, s, s), bf16),
            jax.ShapeDtypeStruct((2, count // 2, s, s), f32),
            jax.ShapeDtypeStruct((count, s), f32),
            jax.ShapeDtypeStruct((2, s + PAD, s), f32),
        ],
        scratch_shapes=[pltpu.VMEM((2, s + PAD, s), f32)],
        name="local_maps",
    )(decay, observed, halves(coupling), halves(obs_map), halves(gain))


def scan_kernel(steps, decay_ref, var_ref, factor_ref, map_ref, gain_ref, step_ref, total_ref,
                mean0_ref, var0_ref, shift_ref, maps_ref, mean_ref, out_ref,
                noise, obs_var, base, base_half, diag, own_map, own_part,
                map_x, map_z, map_y, part_x, part_z, part_y,
                later, before, pair_map, pair_part, state, entry, maps_here, off, straight,
                first_mean, send_sem, recv_sem, pair_sem, maps_sem):
    i = pl.program_id(0)
    last = pl.num_programs(0) - 1
    row, col = lax.axis_index("row"), lax.axis_index("col")
    y, z = row // 4, lax.rem(row, 4)
    x, core = col // 2, lax.rem(col, 2)
    s = decay_ref.shape[1]
    half = decay_ref.shape[0] // 2

    def step(p, by):
        return lax.rem(p + by, 4)

    def along_x(by):
        return (row, step(x, by) * 2 + core)

    def along_z(by):
        return (y * 4 + step(z, by), col)

    def along_y(by):
        return (step(y, by) * 4 + z, col)

    partner = (row, x * 2 + 1 - core)

    def on_chip(source, target, k):
        return pltpu.make_async_remote_copy(
            src_ref=source, dst_ref=target, send_sem=pair_sem.at[0, k],
            recv_sem=pair_sem.at[1, k], device_id=partner, device_id_type=MESH_ID)

    def copy(level, kind, hold, p, along, by, source=0):
        slot = step(p, source)
        return pltpu.make_async_remote_copy(
            src_ref=hold.at[slot], dst_ref=hold.at[slot],
            send_sem=send_sem.at[level, kind, by - 1], recv_sem=recv_sem.at[level, kind, by - 1],
            device_id=along(by), device_id_type=MESH_ID)

    class Ring:
        def __init__(self, *what):
            self.what = what
            self.hold, self.p = what[2], what[3]

        def start(self):
            for by in (1, 3, 2):
                copy(*self.what, by).start()

        def arrived(self, by):
            copy(*self.what, by, source=4 - by).wait_recv()
            return step(self.p, 4 - by)

        def drain(self):
            for by in (1, 3, 2):
                copy(*self.what, by).wait_send()

    mx, px = Ring(0, 0, map_x, x, along_x), Ring(0, 1, part_x, x, along_x)
    mz, pz = Ring(1, 0, map_z, z, along_z), Ring(1, 1, part_z, z, along_z)
    my, py = Ring(2, 0, map_y, y, along_y), Ring(2, 1, part_y, y, along_y)

    @pl.when(i == 0)
    def _():
        barrier = pltpu.get_barrier_semaphore()
        pl.semaphore_signal(barrier, inc=1, device_id=partner, device_id_type=MESH_ID)
        for along in (along_x, along_z, along_y):
            for by in (1, 2, 3):
                pl.semaphore_signal(barrier, inc=1, device_id=along(by), device_id_type=MESH_ID)
        noise[...] = jnp.zeros_like(noise)
        obs_var[...] = jnp.broadcast_to(var_ref[...] * 0.5, obs_var.shape[::-1]).T
        own_map[...] = product(total_ref[0, :s], total_ref[1, :s])
        q = dot_nt(factor_ref[...], factor_ref[...])
        base[...] = q
        base_half[...] = q.astype(bf16)
        pl.semaphore_wait(barrier, 10)
        on_chip(own_map, pair_map, 0).start()

    fetch = pltpu.make_async_copy(maps_ref, maps_here, maps_sem.at[0])

    @pl.when(i == 1)
    def _():
        fetch.start()
        on_chip(own_map, pair_map, 0).wait_recv()

    @pl.when(jnp.logical_and(i == 1, core == 0))
    def _():
        map_x[x] = product(own_map[...], pair_map[...])
        mx.start()

    diagonal = eye(s)
    m = map_ref.shape[2]
    seen_all = dot_nn(map_ref[...].reshape(-1, s), base_half[...])

    def build(h, j):
        t = h * half + i * steps + j
        k = h * steps + j
        obs_map, gain = map_ref[h, j], gain_ref[h, j]
        seen = seen_all[k * m:(k + 1) * m]
        inner = (dot_nt(obs_map, seen.astype(bf16)) * 0.5).astype(bf16)
        fresh = (dot_nn(inner, gain) + gain.astype(f32) * obs_var[:, 0:1] - seen).astype(bf16)
        decay = decay_ref[pl.ds(t, 1), :]
        decay_t = jnp.broadcast_to(decay, (8, s)).T[:, 0:1]
        left = jnp.concatenate([gain, fresh], axis=0).T
        return t, decay, decay_t, left, jnp.concatenate([fresh, gain], axis=0)

    ns = [noise[0], noise[1]]
    ready = [build(0, 0), build(1, 0)]
    for j in range(steps):
        for h in range(2):
            t, decay, decay_t, left, right = ready[h]
            e = step_ref[h, j]
            v = ns[h] * decay + dot_nt(ns[h].astype(bf16), e)
            if j + 1 < steps:
                ready[h] = build(h, j + 1)
            pushed = dot_nn(jnp.concatenate([e, left], axis=1),
                            jnp.concatenate([v.astype(bf16), right], axis=0))
            n = v * decay_t + base[...] + pushed
            diag[pl.ds(t, 1), :] = jnp.sum(jnp.where(diagonal, n, 0.0), axis=0, keepdims=True)
            ns[h] = n
    for h in range(2):
        noise[h] = ns[h]

    def pairs(maps):
        m01 = product(maps[0], maps[1])
        m23 = product(maps[2], maps[3])
        return m01, m23

    def suffixes(maps, m23):
        later[3] = jnp.where(eye(s), 1.0, 0.0).astype(f32)
        later[2] = maps[3]
        later[1] = m23
        later[0] = product(maps[1], m23)

    def earlier_map(p, maps, m01):
        m012 = product(m01, maps[2])
        unit = jnp.where(eye(s), 1.0, 0.0).astype(f32)
        low = jnp.where(p == 0, unit, maps[0])
        return jnp.where(p < 2, low, jnp.where(p == 2, m01, m012))

    def earlier_part(p, parts, maps):
        p0 = unpack(parts[0])
        p01 = moved(p0, maps[1]) + unpack(parts[1])
        p012 = moved(p01, maps[2]) + unpack(parts[2])
        low = jnp.where(p == 0, 0.0, p0)
        return jnp.where(p < 2, low, jnp.where(p == 2, p01, p012))

    def total_part(ring, p):
        parts = ring.hold
        sum_ = moved(unpack(parts[p]), later[p])
        left, right = ring.arrived(1), ring.arrived(3)
        sum_ = sum_ + moved(unpack(parts[left]), later[left])
        sum_ = sum_ + moved(unpack(parts[right]), later[right])
        across = ring.arrived(2)
        return pack(sum_ + moved(unpack(parts[across]), later[across]))

    def first_half():
        return jnp.concatenate([noise[0], total_ref[0, s:]], axis=0)

    def second_half():
        return jnp.concatenate([noise[1], total_ref[1, s:]], axis=0)

    @pl.when(jnp.logical_and(i == last, core == 1))
    def _():
        own_part[...] = moved(first_half(), total_ref[1, :s]) + second_half()
        on_chip(own_part, pair_part, 1).start()
        before[0] = product(pair_map[...], total_ref[0, :s])
        on_chip(own_part, pair_part, 1).wait_recv()
        part = pair_part[...]
        kept = moved(part, total_ref[0, :s]) + first_half()
        on_chip(state, state, 2).wait_recv()
        near = unpack(state[...])
        entry[0] = moved(near, pair_map[...]) + pair_part[...]
        entry[1] = moved(near, before[0]) + kept

    @pl.when(jnp.logical_and(i == last, core == 0))
    def _():
        for by in (1, 3, 2):
            mx.arrived(by)
        x01, x23 = pairs(map_x)
        map_z[z] = product(x01, x23)
        mz.start()
        far = product(total_ref[1, :s], pair_map[...])
        mine = moved(first_half(), far) + moved(second_half(), pair_map[...])
        on_chip(own_part, pair_part, 1).wait_recv()
        part_x[x] = pack(mine + pair_part[...])
        px.start()
        suffixes(map_x, x23)
        own_part[...] = moved(first_half(), total_ref[1, :s]) + second_half()
        on_chip(own_part, pair_part, 1).start()
        before[0] = earlier_map(x, map_x, x01)
        part_z[z] = total_part(px, x)
        pz.start()
        for by in (1, 3, 2):
            mz.arrived(by)
        z01, z23 = pairs(map_z)
        map_y[y] = product(z01, z23)
        my.start()
        suffixes(map_z, z23)
        near = earlier_part(x, part_x, map_x)
        before[3] = product(earlier_map(z, map_z, z01), before[0])
        part_y[y] = total_part(pz, z)
        py.start()
        near = near + moved(earlier_part(z, part_z, map_z), before[0])
        for by in (1, 3, 2):
            my.arrived(by)
        for q in (2, 1, 0):
            after = before[q + 1]
            before[q] = jnp.where(q < y, product(map_y[q], after), after)
        t0 = before[0]
        weights = jnp.broadcast_to(var0_ref[...], (8, s)).T[:, 0:1]
        u_hi, u_lo = split(t0)
        w_hi, w_lo = split(t0 * weights)
        u_hi_t, u_lo_t = u_hi.T, u_lo.T
        start_noise = dot_nn(u_hi_t, w_hi) + (dot_nn(u_hi_t, w_lo) + dot_nn(u_lo_t, w_hi))
        start_mean = product(jnp.broadcast_to(mean0_ref[...], (PAD, s)), t0)
        near = near + jnp.concatenate([start_noise, start_mean], axis=0)
        for by in (1, 3, 2):
            q = py.arrived(by)
            part = moved(unpack(part_y[q]), before[jnp.minimum(q + 1, 3)])
            near = near + jnp.where(q < y, part, 0.0)
        state[...] = pack(near)
        on_chip(state, state, 2).start()
        entry[0] = near
        entry[1] = moved(near, total_ref[0, :s]) + first_half()

    @pl.when(i == last)
    def _():
        for h in range(2):
            cov = entry[h, :s]
            off[h] = jnp.where(diagonal, 0.0, cov).astype(bf16)
            held = jnp.sum(jnp.where(diagonal, cov, 0.0), axis=1, keepdims=True)
            straight[h] = jnp.broadcast_to(held, (s, s))
            first_mean[h] = jnp.broadcast_to(entry[h, s:s + 8].T[:, 0:1], (s, s))
        fetch.wait()

        @pl.loop(0, half // steps)
        def _(block):
            for j in range(steps):
                for h in range(2):
                    k = block * steps + j
                    t = h * half + k
                    maps = maps_here[h, k]
                    r = dot_nn(off[h], maps.astype(bf16)) + straight[h] * maps
                    out_ref[pl.ds(t, 1), :] = (
                        jnp.sum(r * maps, axis=0, keepdims=True) + diag[pl.ds(t, 1), :]
                    )
                    mean_ref[pl.ds(t, 1), :] = (
                        jnp.sum(first_mean[h] * maps, axis=0, keepdims=True)
                        + shift_ref[pl.ds(t, 1), :]
                    )

        on_chip(own_map, pair_map, 0).wait_send()
        on_chip(own_part, pair_part, 1).wait_send()

    @pl.when(jnp.logical_and(i == last, core == 0))
    def _():
        for ring in (mx, px, mz, pz, my, py):
            ring.drain()
        on_chip(state, state, 2).wait_send()


def scan(decay, obs_var, factor, obs_map, gain, step_maps, total, init_mean, init_var, shift, maps):
    count, s = decay.shape
    m = obs_map.shape[1]
    steps = SPB
    rows = s + PAD
    packed = s // 2 + s // 4 + 8
    block = lambda i: (0, i, 0, 0)
    flat = pl.BlockSpec((2, steps, m, s), block)
    three = lambda i: (0, 0, 0)
    return pl.pallas_call(
        functools.partial(scan_kernel, steps),
        grid=(count // (2 * steps),),
        in_specs=[
            pl.BlockSpec((count, s), whole),
            pl.BlockSpec((1, m), whole),
            pl.BlockSpec((s, s), whole),
            flat,
            flat,
            pl.BlockSpec((2, steps, s, s), block),
            pl.BlockSpec((2, rows, s), three),
            pl.BlockSpec((1, s), whole),
            pl.BlockSpec((1, s), whole),
            pl.BlockSpec((count, s), whole),
            pl.BlockSpec(memory_space=pl.ANY),
        ],
        out_specs=[pl.BlockSpec((count, s), whole)] * 2,
        out_shape=[jax.ShapeDtypeStruct((count, s), f32)] * 2,
        scratch_shapes=[
            pltpu.VMEM((2, s, s), f32),
            pltpu.VMEM((m, 8), f32),
            pltpu.VMEM((s, s), f32),
            pltpu.VMEM((s, s), bf16),
            pltpu.VMEM((count, s), f32),
            pltpu.VMEM((s, s), f32),
            pltpu.VMEM((rows, s), f32),
        ] + [pltpu.VMEM((4, s, s), f32)] * 3 + [pltpu.VMEM((4, packed, s), f32)] * 3 + [
            pltpu.VMEM((4, s, s), f32),
            pltpu.VMEM((4, s, s), f32),
            pltpu.VMEM((s, s), f32),
            pltpu.VMEM((rows, s), f32),
            pltpu.VMEM((packed, s), f32),
            pltpu.VMEM((2, rows, s), f32),
            pltpu.VMEM((2, count // 2, s, s), f32),
            pltpu.VMEM((2, s, s), bf16),
            pltpu.VMEM((2, s, s), f32),
            pltpu.VMEM((2, s, s), f32),
            pltpu.SemaphoreType.DMA((3, 2, 3)),
            pltpu.SemaphoreType.DMA((3, 2, 3)),
            pltpu.SemaphoreType.DMA((2, 3)),
            pltpu.SemaphoreType.DMA((1,)),
        ],
        compiler_params=pltpu.CompilerParams(collective_id=0, has_side_effects=True),
        name="scan_devices",
    )(decay, obs_var[None, :], factor, halves(obs_map), halves(gain), step_maps, total,
      init_mean[None, :], init_var[None, :], shift, maps)


def per_device(
    init_mean, init_var, decay, coupling, obs_map, gain, noise_factor, obs_var, observed
):
    step_maps, maps, shift, total = local_maps(decay, coupling, obs_map, gain, observed)
    means, variances = scan(
        decay, obs_var, noise_factor, obs_map, gain, step_maps, total, init_mean, init_var,
        shift, maps,
    )
    return (means, variances)


def solution(mesh):
    return jax.shard_map(
        per_device,
        mesh=mesh,
        in_specs=(
            P(),
            P(),
            P(("row", "col"), None),
            P(("row", "col"), None, None),
            P(("row", "col"), None, None),
            P(("row", "col"), None, None),
            P(),
            P(),
            P(("row", "col"), None),
        ),
        out_specs=(P(("row", "col"), None), P(("row", "col"), None)),
        check_vma=False,
    )
```

```python
import functools

import jax
import jax.numpy as jnp
from jax import lax
from jax.experimental import pallas as pl
from jax.experimental.pallas import tpu as pltpu
from jax.sharding import PartitionSpec as P

f32 = jnp.float32
bf16 = jnp.bfloat16
PAD = 16
SPB = 4


def dot_nn(a, b):
    return lax.dot_general(a, b, (((1,), (0,)), ((), ())), preferred_element_type=f32)


def dot_nt(a, b):
    return lax.dot_general(a, b, (((1,), (1,)), ((), ())), preferred_element_type=f32)


def split(x):
    hi = x.astype(bf16)
    return hi, (x - hi.astype(f32)).astype(bf16)


def eye(n):
    row = lax.broadcasted_iota(jnp.int32, (n, n), 0)
    col = lax.broadcasted_iota(jnp.int32, (n, n), 1)
    return row == col


MESH_ID = pl.DeviceIdType.MESH


def product(a, b):
    a_hi, a_lo = split(a)
    b_hi, b_lo = split(b)
    return dot_nn(a_hi, b_hi) + (dot_nn(a_lo, b_hi) + dot_nn(a_hi, b_lo))


def moved(part, maps):
    s = maps.shape[0]
    t_hi, t_lo = split(maps)
    x_hi, x_lo = split(part)
    y = dot_nn(x_hi, t_hi) + (dot_nn(x_lo, t_hi) + dot_nn(x_hi, t_lo))
    v_hi, v_lo = split(y[:s])
    u_hi, u_lo = t_hi.T, t_lo.T
    n = dot_nn(u_hi, v_hi) + (dot_nn(u_hi, v_lo) + dot_nn(u_lo, v_hi))
    return jnp.concatenate([n, y[s:]], axis=0)


def pack(part):
    s = part.shape[1]
    h, k = s // 2, s // 4
    square = jnp.concatenate([part[h:h + k, h:], part[h + k:s, h:]], axis=1)
    return jnp.concatenate([part[:h], square, part[s:s + 8]], axis=0)


def unpack(packed):
    s = packed.shape[1]
    h, k = s // 2, s // 4
    top, square, shift = packed[:h], packed[h:h + k], packed[h + k:]
    corner = jnp.concatenate([square[:, :h], square[:, h:]], axis=0)
    low = jnp.concatenate([top[:, h:].T, corner], axis=1)
    return jnp.concatenate([top, low] + [shift] * (PAD // 8), axis=0)


def maps_kernel(steps, decay_ref, observed_ref, coupling_ref, map_ref, gain_ref,
                step_ref, maps_ref, shift_ref, total_ref, state):
    i = pl.program_id(0)
    s = decay_ref.shape[1]
    half = decay_ref.shape[0] // 2

    @pl.when(i == 0)
    def _():
        unit = jnp.where(eye(s), 1.0, 0.0).astype(f32)
        for h in range(2):
            state[h] = jnp.concatenate([unit, jnp.zeros((PAD, s), f32)], axis=0)

    def build(h, j):
        t = h * half + i * steps + j
        decay = decay_ref[pl.ds(t, 1), :]
        obs_map, gain, coupling = map_ref[h, j], gain_ref[h, j], coupling_ref[h, j]
        obs_f = (obs_map.astype(f32) * decay + dot_nn(obs_map, coupling)).astype(bf16)
        e_hi, e_lo = split(coupling.astype(f32) - dot_nn(gain.T, obs_f))
        step_ref[h, j] = e_hi
        z_hi, z_lo = split(jnp.broadcast_to(observed_ref[pl.ds(t, 1), :], (PAD, gain.shape[0])))
        both = dot_nn(jnp.concatenate([z_hi, z_lo], axis=0), gain)
        return t, decay, e_hi, e_lo, both[:PAD] + both[PAD:]

    maps = [state[0], state[1]]
    ready = [build(0, 0), build(1, 0)]
    for j in range(steps):
        for h in range(2):
            t, decay, e_hi, e_lo, shift = ready[h]
            m_hi, m_lo = split(maps[h])
            moved = dot_nt(jnp.concatenate([m_hi, m_lo], axis=0), e_hi)
            y = maps[h] * decay + (moved[:s + PAD] + (moved[s + PAD:] + dot_nt(m_hi, e_lo)))
            b = y[s:] + shift
            maps_ref[h, j] = y[:s]
            shift_ref[pl.ds(t, 1), :] = b[0:1]
            maps[h] = jnp.concatenate([y[:s], b], axis=0)
            if j + 1 < steps:
                ready[h] = build(h, j + 1)
    for h in range(2):
        state[h] = maps[h]

    @pl.when(i == pl.num_programs(0) - 1)
    def _():
        total_ref[...] = state[...]


def halves(a):
    return a.reshape((2, a.shape[0] // 2) + a.shape[1:])


def whole(i):
    return (0, 0)


def local_maps(decay, coupling, obs_map, gain, observed):
    count, s = decay.shape
    m = obs_map.shape[1]
    steps = SPB
    block = lambda i: (0, i, 0, 0)
    square = pl.BlockSpec((2, steps, s, s), block)
    flat = pl.BlockSpec((2, steps, m, s), block)
    return pl.pallas_call(
        functools.partial(maps_kernel, steps),
        grid=(count // (2 * steps),),
        in_specs=[pl.BlockSpec((count, s), whole), pl.BlockSpec((count, m), whole),
                  square, flat, flat],
        out_specs=[square, square, pl.BlockSpec((count, s), whole),
                   pl.BlockSpec((2, s + PAD, s), lambda i: (0, 0, 0))],
        out_shape=[
            jax.ShapeDtypeStruct((2, count // 2, s, s), bf16),
            jax.ShapeDtypeStruct((2, count // 2, s, s), f32),
            jax.ShapeDtypeStruct((count, s), f32),
            jax.ShapeDtypeStruct((2, s + PAD, s), f32),
        ],
        scratch_shapes=[pltpu.VMEM((2, s + PAD, s), f32)],
        name="local_maps",
    )(decay, observed, halves(coupling), halves(obs_map), halves(gain))


def scan_kernel(steps, decay_ref, var_ref, factor_ref, map_ref, gain_ref, step_ref, total_ref,
                mean0_ref, var0_ref, shift_ref, maps_ref, out_ref,
                noise, obs_var, base, base_half, diag, own_map, own_part,
                map_x, map_z, map_y, part_x, part_z, part_y,
                later, before, pair_map, pair_part, state, entry, maps_here, off, straight,
                first_mean, send_sem, recv_sem, pair_sem, maps_sem):
    i = pl.program_id(0)
    last = pl.num_programs(0) - 1
    row, col = lax.axis_index("row"), lax.axis_index("col")
    y, z = row // 4, lax.rem(row, 4)
    x, core = col // 2, lax.rem(col, 2)
    s = decay_ref.shape[1]
    half = decay_ref.shape[0] // 2

    def step(p, by):
        return lax.rem(p + by, 4)

    def along_x(by):
        return (row, step(x, by) * 2 + core)

    def along_z(by):
        return (y * 4 + step(z, by), col)

    def along_y(by):
        return (step(y, by) * 4 + z, col)

    partner = (row, x * 2 + 1 - core)

    def on_chip(source, target, k):
        return pltpu.make_async_remote_copy(
            src_ref=source, dst_ref=target, send_sem=pair_sem.at[0, k],
            recv_sem=pair_sem.at[1, k], device_id=partner, device_id_type=MESH_ID)

    class Ring:
        def __init__(self, level, kind, hold, p, along):
            self.sem, self.hold, self.p = (level, kind), hold, p
            self.right, self.left = along(1), along(3)
            rows = hold.shape[1]
            q = rows // 32 * 8
            self.cut = [(0, rows - 3 * q)] + [(rows - k * q, q) for k in (3, 2, 1)]

        def piece(self, source, k, sem, target):
            rows = pl.ds(*self.cut[k])
            slot = step(self.p, source)
            return pltpu.make_async_remote_copy(
                src_ref=self.hold.at[slot, rows], dst_ref=self.hold.at[slot, rows],
                send_sem=send_sem.at[(*self.sem, sem)], recv_sem=recv_sem.at[(*self.sem, sem)],
                device_id=target, device_id_type=MESH_ID)

        def start(self):
            for k in range(4):
                self.piece(0, k, k, self.right).start()
                other = (k + 2) % 4
                self.piece(0, other, 4 + other, self.left).start()

        def relay(self):
            for k in range(2):
                self.piece(3, k, k, self.right).wait_recv()
                self.piece(3, k, 8 + k, self.right).start()
                self.piece(1, k + 2, 6 + k, self.left).wait_recv()
                self.piece(1, k + 2, 10 + k, self.left).start()

        def neighbours(self):
            for k in range(2):
                self.piece(3, k + 2, k + 2, self.right).wait_recv()
                self.piece(1, k, 4 + k, self.left).wait_recv()
            return step(self.p, 3), step(self.p, 1)

        def across(self):
            for k in range(2):
                self.piece(2, k, 8 + k, self.right).wait_recv()
                self.piece(2, k + 2, 10 + k, self.left).wait_recv()
            return step(self.p, 2)

        def drain(self):
            for k in range(4):
                self.piece(0, k, k, self.right).wait_send()
                self.piece(0, k, 4 + k, self.left).wait_send()
            for k in range(2):
                self.piece(3, k, 8 + k, self.right).wait_send()
                self.piece(1, k + 2, 10 + k, self.left).wait_send()

    mx, px = Ring(0, 0, map_x, x, along_x), Ring(0, 1, part_x, x, along_x)
    mz, pz = Ring(1, 0, map_z, z, along_z), Ring(1, 1, part_z, z, along_z)
    my, py = Ring(2, 0, map_y, y, along_y), Ring(2, 1, part_y, y, along_y)

    @pl.when(i == 0)
    def _():
        barrier = pltpu.get_barrier_semaphore()
        pl.semaphore_signal(barrier, inc=1, device_id=partner, device_id_type=MESH_ID)
        for along in (along_x, along_z, along_y):
            for by in (1, 3):
                pl.semaphore_signal(barrier, inc=1, device_id=along(by), device_id_type=MESH_ID)
        noise[...] = jnp.zeros_like(noise)
        obs_var[...] = jnp.broadcast_to(var_ref[...] * 0.5, obs_var.shape[::-1]).T
        own_map[...] = product(total_ref[0, :s], total_ref[1, :s])
        q = dot_nt(factor_ref[...], factor_ref[...])
        base[...] = q
        base_half[...] = q.astype(bf16)
        pl.semaphore_wait(barrier, 7)
        on_chip(own_map, pair_map, 0).start()

    fetch = pltpu.make_async_copy(maps_ref, maps_here, maps_sem.at[0])

    @pl.when(i == 1)
    def _():
        fetch.start()
        on_chip(own_map, pair_map, 0).wait_recv()

    @pl.when(jnp.logical_and(i == 1, core == 0))
    def _():
        map_x[x] = product(own_map[...], pair_map[...])
        mx.start()

    @pl.when(jnp.logical_and(i == last, core == 0))
    def _():
        mx.relay()

    diagonal = eye(s)
    m = map_ref.shape[2]
    seen_all = dot_nn(map_ref[...].reshape(-1, s), base_half[...])

    def build(h, j):
        t = h * half + i * steps + j
        k = h * steps + j
        obs_map, gain = map_ref[h, j], gain_ref[h, j]
        seen = seen_all[k * m:(k + 1) * m]
        inner = (dot_nt(obs_map, seen.astype(bf16)) * 0.5).astype(bf16)
        fresh = (dot_nn(inner, gain) + gain.astype(f32) * obs_var[:, 0:1] - seen).astype(bf16)
        decay = decay_ref[pl.ds(t, 1), :]
        decay_t = jnp.broadcast_to(decay, (8, s)).T[:, 0:1]
        left = jnp.concatenate([gain, fresh], axis=0).T
        return t, decay, decay_t, left, jnp.concatenate([fresh, gain], axis=0)

    ns = [noise[0], noise[1]]
    ready = [build(0, 0), build(1, 0)]
    for j in range(steps):
        for h in range(2):
            t, decay, decay_t, left, right = ready[h]
            e = step_ref[h, j]
            v = ns[h] * decay + dot_nt(ns[h].astype(bf16), e)
            if j + 1 < steps:
                ready[h] = build(h, j + 1)
            pushed = dot_nn(jnp.concatenate([e, left], axis=1),
                            jnp.concatenate([v.astype(bf16), right], axis=0))
            n = v * decay_t + base[...] + pushed
            diag[pl.ds(t, 1), :] = jnp.sum(jnp.where(diagonal, n, 0.0), axis=0, keepdims=True)
            ns[h] = n
    for h in range(2):
        noise[h] = ns[h]

    def pairs(maps):
        m01 = product(maps[0], maps[1])
        m23 = product(maps[2], maps[3])
        return m01, m23

    def suffixes(maps, m23):
        later[3] = jnp.where(eye(s), 1.0, 0.0).astype(f32)
        later[2] = maps[3]
        later[1] = m23
        later[0] = product(maps[1], m23)

    def earlier_map(p, maps, m01):
        m012 = product(m01, maps[2])
        unit = jnp.where(eye(s), 1.0, 0.0).astype(f32)
        low = jnp.where(p == 0, unit, maps[0])
        return jnp.where(p < 2, low, jnp.where(p == 2, m01, m012))

    def earlier_part(p, parts, maps):
        p0 = unpack(parts[0])
        p01 = moved(p0, maps[1]) + unpack(parts[1])
        p012 = moved(p01, maps[2]) + unpack(parts[2])
        low = jnp.where(p == 0, 0.0, p0)
        return jnp.where(p < 2, low, jnp.where(p == 2, p01, p012))

    def total_part(ring, p):
        parts = ring.hold
        sum_ = moved(unpack(parts[p]), later[p])
        left, right = ring.neighbours()
        sum_ = sum_ + moved(unpack(parts[left]), later[left])
        sum_ = sum_ + moved(unpack(parts[right]), later[right])
        across = ring.across()
        return pack(sum_ + moved(unpack(parts[across]), later[across]))

    def first_half():
        return jnp.concatenate([noise[0], total_ref[0, s:]], axis=0)

    def second_half():
        return jnp.concatenate([noise[1], total_ref[1, s:]], axis=0)

    @pl.when(jnp.logical_and(i == last, core == 1))
    def _():
        own_part[...] = moved(first_half(), total_ref[1, :s]) + second_half()
        on_chip(own_part, pair_part, 1).start()
        before[0] = product(pair_map[...], total_ref[0, :s])
        on_chip(own_part, pair_part, 1).wait_recv()
        part = pair_part[...]
        kept = moved(part, total_ref[0, :s]) + first_half()
        on_chip(state, state, 2).wait_recv()
        near = unpack(state[...])
        entry[0] = moved(near, pair_map[...]) + pair_part[...]
        entry[1] = moved(near, before[0]) + kept

    @pl.when(jnp.logical_and(i == last, core == 0))
    def _():
        far = product(total_ref[1, :s], pair_map[...])
        mine = moved(first_half(), far) + moved(second_half(), pair_map[...])
        on_chip(own_part, pair_part, 1).wait_recv()
        part_x[x] = pack(mine + pair_part[...])
        px.start()
        mx.neighbours()
        mx.across()
        x01, x23 = pairs(map_x)
        map_z[z] = product(x01, x23)
        mz.start()
        suffixes(map_x, x23)
        px.relay()
        own_part[...] = moved(first_half(), total_ref[1, :s]) + second_half()
        on_chip(own_part, pair_part, 1).start()
        mz.relay()
        before[0] = earlier_map(x, map_x, x01)
        part_z[z] = total_part(px, x)
        pz.start()
        mz.neighbours()
        mz.across()
        z01, z23 = pairs(map_z)
        map_y[y] = product(z01, z23)
        my.start()
        suffixes(map_z, z23)
        pz.relay()
        near = earlier_part(x, part_x, map_x)
        my.relay()
        before[3] = product(earlier_map(z, map_z, z01), before[0])
        part_y[y] = total_part(pz, z)
        py.start()
        near = near + moved(earlier_part(z, part_z, map_z), before[0])
        py.relay()
        my.neighbours()
        my.across()
        for q in (2, 1, 0):
            after = before[q + 1]
            before[q] = jnp.where(q < y, product(map_y[q], after), after)
        t0 = before[0]
        weights = jnp.broadcast_to(var0_ref[...], (8, s)).T[:, 0:1]
        u_hi, u_lo = split(t0)
        w_hi, w_lo = split(t0 * weights)
        u_hi_t, u_lo_t = u_hi.T, u_lo.T
        start_noise = dot_nn(u_hi_t, w_hi) + (dot_nn(u_hi_t, w_lo) + dot_nn(u_lo_t, w_hi))
        start_mean = product(jnp.broadcast_to(mean0_ref[...], (PAD, s)), t0)
        near = near + jnp.concatenate([start_noise, start_mean], axis=0)

        def slab(q):
            part = moved(unpack(part_y[q]), before[jnp.minimum(q + 1, 3)])
            return jnp.where(q < y, part, 0.0)

        left, right = py.neighbours()
        near = near + slab(left) + slab(right)
        near = near + slab(py.across())
        state[...] = pack(near)
        on_chip(state, state, 2).start()
        entry[0] = near
        entry[1] = moved(near, total_ref[0, :s]) + first_half()

    @pl.when(i == last)
    def _():
        for h in range(2):
            cov = entry[h, :s]
            off[h] = jnp.where(diagonal, 0.0, cov).astype(bf16)
            held = jnp.sum(jnp.where(diagonal, cov, 0.0), axis=1, keepdims=True)
            straight[h] = jnp.broadcast_to(held, (s, s))
            first_mean[h] = jnp.broadcast_to(entry[h, s:s + 8].T[:, 0:1], (s, s))
        fetch.wait()

        @pl.loop(0, half // steps)
        def _(block):
            for j in range(steps):
                for h in range(2):
                    k = block * steps + j
                    t = h * half + k
                    maps = maps_here[h, k]
                    r = dot_nn(off[h], maps.astype(bf16)) + straight[h] * maps
                    out_ref[1, pl.ds(t, 1), :] = (
                        jnp.sum(r * maps, axis=0, keepdims=True) + diag[pl.ds(t, 1), :]
                    )
                    out_ref[0, pl.ds(t, 1), :] = (
                        jnp.sum(first_mean[h] * maps, axis=0, keepdims=True)
                        + shift_ref[pl.ds(t, 1), :]
                    )

        on_chip(own_map, pair_map, 0).wait_send()
        on_chip(own_part, pair_part, 1).wait_send()

    @pl.when(jnp.logical_and(i == last, core == 0))
    def _():
        for ring in (mx, px, mz, pz, my, py):
            ring.drain()
        on_chip(state, state, 2).wait_send()


def scan(decay, obs_var, factor, obs_map, gain, step_maps, total, init_mean, init_var, shift, maps):
    count, s = decay.shape
    m = obs_map.shape[1]
    steps = SPB
    rows = s + PAD
    packed = s // 2 + s // 4 + 8
    block = lambda i: (0, i, 0, 0)
    flat = pl.BlockSpec((2, steps, m, s), block)
    three = lambda i: (0, 0, 0)
    return pl.pallas_call(
        functools.partial(scan_kernel, steps),
        grid=(count // (2 * steps),),
        in_specs=[
            pl.BlockSpec((count, s), whole),
            pl.BlockSpec((1, m), whole),
            pl.BlockSpec((s, s), whole),
            flat,
            flat,
            pl.BlockSpec((2, steps, s, s), block),
            pl.BlockSpec((2, rows, s), three),
            pl.BlockSpec((1, s), whole),
            pl.BlockSpec((1, s), whole),
            pl.BlockSpec((count, s), whole),
            pl.BlockSpec(memory_space=pl.ANY),
        ],
        out_specs=pl.BlockSpec((2, count, s), three),
        out_shape=jax.ShapeDtypeStruct((2, count, s), f32),
        scratch_shapes=[
            pltpu.VMEM((2, s, s), f32),
            pltpu.VMEM((m, 8), f32),
            pltpu.VMEM((s, s), f32),
            pltpu.VMEM((s, s), bf16),
            pltpu.VMEM((count, s), f32),
            pltpu.VMEM((s, s), f32),
            pltpu.VMEM((rows, s), f32),
        ] + [pltpu.VMEM((4, s, s), f32)] * 3 + [pltpu.VMEM((4, packed, s), f32)] * 3 + [
            pltpu.VMEM((4, s, s), f32),
            pltpu.VMEM((4, s, s), f32),
            pltpu.VMEM((s, s), f32),
            pltpu.VMEM((rows, s), f32),
            pltpu.VMEM((packed, s), f32),
            pltpu.VMEM((2, rows, s), f32),
            pltpu.VMEM((2, count // 2, s, s), f32),
            pltpu.VMEM((2, s, s), bf16),
            pltpu.VMEM((2, s, s), f32),
            pltpu.VMEM((2, s, s), f32),
            pltpu.SemaphoreType.DMA((3, 2, 12)),
            pltpu.SemaphoreType.DMA((3, 2, 12)),
            pltpu.SemaphoreType.DMA((2, 3)),
            pltpu.SemaphoreType.DMA((1,)),
        ],
        compiler_params=pltpu.CompilerParams(collective_id=0, has_side_effects=True),
        name="scan_devices",
    )(decay, obs_var[None, :], factor, halves(obs_map), halves(gain), step_maps, total,
      init_mean[None, :], init_var[None, :], shift, maps)


def per_device(
    init_mean, init_var, decay, coupling, obs_map, gain, noise_factor, obs_var, observed
):
    step_maps, maps, shift, total = local_maps(decay, coupling, obs_map, gain, observed)
    both = scan(
        decay, obs_var, noise_factor, obs_map, gain, step_maps, total, init_mean, init_var,
        shift, maps,
    )
    return (both[0], both[1])


def solution(mesh):
    return jax.shard_map(
        per_device,
        mesh=mesh,
        in_specs=(
            P(),
            P(),
            P(("row", "col"), None),
            P(("row", "col"), None, None),
            P(("row", "col"), None, None),
            P(("row", "col"), None, None),
            P(),
            P(),
            P(("row", "col"), None),
        ),
        out_specs=(P(("row", "col"), None), P(("row", "col"), None)),
        check_vma=False,
    )
```

```python
import functools

import jax
import jax.numpy as jnp
from jax import lax
from jax.experimental import pallas as pl
from jax.experimental.pallas import tpu as pltpu
from jax.sharding import PartitionSpec as P

f32 = jnp.float32
bf16 = jnp.bfloat16
PAD = 16
SPB = 4
SPN = 8


def dot_nn(a, b):
    return lax.dot_general(a, b, (((1,), (0,)), ((), ())), preferred_element_type=f32)


def dot_nt(a, b):
    return lax.dot_general(a, b, (((1,), (1,)), ((), ())), preferred_element_type=f32)


def split(x):
    hi = x.astype(bf16)
    return hi, (x - hi.astype(f32)).astype(bf16)


def eye(n):
    row = lax.broadcasted_iota(jnp.int32, (n, n), 0)
    col = lax.broadcasted_iota(jnp.int32, (n, n), 1)
    return row == col


MESH_ID = pl.DeviceIdType.MESH


def product(a, b):
    a_hi, a_lo = split(a)
    b_hi, b_lo = split(b)
    return dot_nn(a_hi, b_hi) + (dot_nn(a_lo, b_hi) + dot_nn(a_hi, b_lo))


def moved(part, maps):
    s = maps.shape[0]
    t_hi, t_lo = split(maps)
    x_hi, x_lo = split(part)
    y = dot_nn(x_hi, t_hi) + (dot_nn(x_lo, t_hi) + dot_nn(x_hi, t_lo))
    v_hi, v_lo = split(y[:s])
    u_hi, u_lo = t_hi.T, t_lo.T
    n = dot_nn(u_hi, v_hi) + (dot_nn(u_hi, v_lo) + dot_nn(u_lo, v_hi))
    return jnp.concatenate([n, y[s:]], axis=0)


def pack(part):
    s = part.shape[1]
    h, k = s // 2, s // 4
    square = jnp.concatenate([part[h:h + k, h:], part[h + k:s, h:]], axis=1)
    return jnp.concatenate([part[:h], square, part[s:s + 8]], axis=0)


def unpack(packed):
    s = packed.shape[1]
    h, k = s // 2, s // 4
    top, square, shift = packed[:h], packed[h:h + k], packed[h + k:]
    corner = jnp.concatenate([square[:, :h], square[:, h:]], axis=0)
    low = jnp.concatenate([top[:, h:].T, corner], axis=1)
    return jnp.concatenate([top, low] + [shift] * (PAD // 8), axis=0)


def maps_kernel(steps, decay_ref, observed_ref, coupling_ref, map_ref, gain_ref,
                step_ref, maps_ref, shift_ref, total_ref, state):
    i = pl.program_id(0)
    s = decay_ref.shape[1]
    half = decay_ref.shape[0] // 2

    @pl.when(i == 0)
    def _():
        unit = jnp.where(eye(s), 1.0, 0.0).astype(f32)
        for h in range(2):
            state[h] = jnp.concatenate([unit, jnp.zeros((PAD, s), f32)], axis=0)

    def build(h, j):
        t = h * half + i * steps + j
        decay = decay_ref[pl.ds(t, 1), :]
        obs_map, gain, coupling = map_ref[h, j], gain_ref[h, j], coupling_ref[h, j]
        obs_f = (obs_map.astype(f32) * decay + dot_nn(obs_map, coupling)).astype(bf16)
        e_hi, e_lo = split(coupling.astype(f32) - dot_nn(gain.T, obs_f))
        step_ref[h, j] = e_hi
        z_hi, z_lo = split(jnp.broadcast_to(observed_ref[pl.ds(t, 1), :], (PAD, gain.shape[0])))
        both = dot_nn(jnp.concatenate([z_hi, z_lo], axis=0), gain)
        return t, decay, e_hi, e_lo, both[:PAD] + both[PAD:]

    maps = [state[0], state[1]]
    ready = [build(0, 0), build(1, 0)]
    for j in range(steps):
        for h in range(2):
            t, decay, e_hi, e_lo, shift = ready[h]
            m_hi, m_lo = split(maps[h])
            moved = dot_nt(jnp.concatenate([m_hi, m_lo], axis=0), e_hi)
            y = maps[h] * decay + (moved[:s + PAD] + (moved[s + PAD:] + dot_nt(m_hi, e_lo)))
            b = y[s:] + shift
            maps_ref[h, j] = y[:s]
            shift_ref[pl.ds(t, 1), :] = b[0:1]
            maps[h] = jnp.concatenate([y[:s], b], axis=0)
            if j + 1 < steps:
                ready[h] = build(h, j + 1)
    for h in range(2):
        state[h] = maps[h]

    @pl.when(i == pl.num_programs(0) - 1)
    def _():
        total_ref[...] = state[...]


def halves(a):
    return a.reshape((2, a.shape[0] // 2) + a.shape[1:])


def whole(i):
    return (0, 0)


def local_maps(decay, coupling, obs_map, gain, observed):
    count, s = decay.shape
    m = obs_map.shape[1]
    steps = SPB
    block = lambda i: (0, i, 0, 0)
    square = pl.BlockSpec((2, steps, s, s), block)
    flat = pl.BlockSpec((2, steps, m, s), block)
    return pl.pallas_call(
        functools.partial(maps_kernel, steps),
        grid=(count // (2 * steps),),
        in_specs=[pl.BlockSpec((count, s), whole), pl.BlockSpec((count, m), whole),
                  square, flat, flat],
        out_specs=[square, square, pl.BlockSpec((count, s), whole),
                   pl.BlockSpec((2, s + PAD, s), lambda i: (0, 0, 0))],
        out_shape=[
            jax.ShapeDtypeStruct((2, count // 2, s, s), bf16),
            jax.ShapeDtypeStruct((2, count // 2, s, s), f32),
            jax.ShapeDtypeStruct((count, s), f32),
            jax.ShapeDtypeStruct((2, s + PAD, s), f32),
        ],
        scratch_shapes=[pltpu.VMEM((2, s + PAD, s), f32)],
        name="local_maps",
    )(decay, observed, halves(coupling), halves(obs_map), halves(gain))


def scan_kernel(steps, decay_ref, var_ref, factor_ref, map_ref, gain_ref, step_ref, total_ref,
                mean0_ref, var0_ref, shift_ref, maps_ref, out_ref,
                noise, obs_var, base, base_half, diag, own_map, own_part,
                map_x, map_z, map_y, part_x, part_z, part_y,
                later, before, pair_map, pair_part, state, entry, maps_here, off, straight,
                first_mean, send_sem, recv_sem, pair_sem, maps_sem):
    i = pl.program_id(0)
    last = pl.num_programs(0) - 1
    row, col = lax.axis_index("row"), lax.axis_index("col")
    y, z = row // 4, lax.rem(row, 4)
    x, core = col // 2, lax.rem(col, 2)
    s = decay_ref.shape[1]
    half = decay_ref.shape[0] // 2

    def step(p, by):
        return lax.rem(p + by, 4)

    def along_x(by):
        return (row, step(x, by) * 2 + core)

    def along_z(by):
        return (y * 4 + step(z, by), col)

    def along_y(by):
        return (step(y, by) * 4 + z, col)

    partner = (row, x * 2 + 1 - core)

    def on_chip(source, target, k):
        return pltpu.make_async_remote_copy(
            src_ref=source, dst_ref=target, send_sem=pair_sem.at[0, k],
            recv_sem=pair_sem.at[1, k], device_id=partner, device_id_type=MESH_ID)

    class Ring:
        def __init__(self, level, kind, hold, p, along):
            self.sem, self.hold, self.p = (level, kind), hold, p
            self.right, self.left = along(1), along(3)
            rows = hold.shape[1]
            q = rows // 32 * 8
            self.cut = [(0, rows - 3 * q)] + [(rows - k * q, q) for k in (3, 2, 1)]

        def piece(self, source, k, sem, target):
            rows = pl.ds(*self.cut[k])
            slot = step(self.p, source)
            return pltpu.make_async_remote_copy(
                src_ref=self.hold.at[slot, rows], dst_ref=self.hold.at[slot, rows],
                send_sem=send_sem.at[(*self.sem, sem)], recv_sem=recv_sem.at[(*self.sem, sem)],
                device_id=target, device_id_type=MESH_ID)

        def start(self):
            for k in range(4):
                self.piece(0, k, k, self.right).start()
                other = (k + 2) % 4
                self.piece(0, other, 4 + other, self.left).start()

        def relay(self):
            for k in range(2):
                self.piece(3, k, k, self.right).wait_recv()
                self.piece(3, k, 8 + k, self.right).start()
                self.piece(1, k + 2, 6 + k, self.left).wait_recv()
                self.piece(1, k + 2, 10 + k, self.left).start()

        def neighbours(self):
            for k in range(2):
                self.piece(3, k + 2, k + 2, self.right).wait_recv()
                self.piece(1, k, 4 + k, self.left).wait_recv()
            return step(self.p, 3), step(self.p, 1)

        def across(self):
            for k in range(2):
                self.piece(2, k, 8 + k, self.right).wait_recv()
                self.piece(2, k + 2, 10 + k, self.left).wait_recv()
            return step(self.p, 2)

        def drain(self):
            for k in range(4):
                self.piece(0, k, k, self.right).wait_send()
                self.piece(0, k, 4 + k, self.left).wait_send()
            for k in range(2):
                self.piece(3, k, 8 + k, self.right).wait_send()
                self.piece(1, k + 2, 10 + k, self.left).wait_send()

    mx, px = Ring(0, 0, map_x, x, along_x), Ring(0, 1, part_x, x, along_x)
    mz, pz = Ring(1, 0, map_z, z, along_z), Ring(1, 1, part_z, z, along_z)
    my, py = Ring(2, 0, map_y, y, along_y), Ring(2, 1, part_y, y, along_y)

    @pl.when(i == 0)
    def _():
        barrier = pltpu.get_barrier_semaphore()
        pl.semaphore_signal(barrier, inc=1, device_id=partner, device_id_type=MESH_ID)
        for along in (along_x, along_z, along_y):
            for by in (1, 3):
                pl.semaphore_signal(barrier, inc=1, device_id=along(by), device_id_type=MESH_ID)
        noise[...] = jnp.zeros_like(noise)
        obs_var[...] = jnp.broadcast_to(var_ref[...] * 0.5, obs_var.shape[::-1]).T
        own_map[...] = product(total_ref[0, :s], total_ref[1, :s])
        q = dot_nt(factor_ref[...], factor_ref[...])
        base[...] = q
        base_half[...] = q.astype(bf16)
        pl.semaphore_wait(barrier, 7)
        on_chip(own_map, pair_map, 0).start()

    fetch = pltpu.make_async_copy(maps_ref, maps_here, maps_sem.at[0])

    @pl.when(i == 1)
    def _():
        fetch.start()
        on_chip(own_map, pair_map, 0).wait_recv()

    @pl.when(jnp.logical_and(i == 1, core == 1))
    def _():
        map_x[x] = product(pair_map[...], own_map[...])
        mx.start()

    diagonal = eye(s)
    m = map_ref.shape[2]
    seen_all = dot_nn(map_ref[...].reshape(-1, s), base_half[...])

    def build(h, j):
        t = h * half + i * steps + j
        k = h * steps + j
        obs_map, gain = map_ref[h, j], gain_ref[h, j]
        seen = seen_all[k * m:(k + 1) * m]
        inner = (dot_nt(obs_map, seen.astype(bf16)) * 0.5).astype(bf16)
        fresh = (dot_nn(inner, gain) + gain.astype(f32) * obs_var[:, 0:1] - seen).astype(bf16)
        decay = decay_ref[pl.ds(t, 1), :]
        decay_t = jnp.broadcast_to(decay, (8, s)).T[:, 0:1]
        left = jnp.concatenate([gain, fresh], axis=0).T
        return t, decay, decay_t, left, jnp.concatenate([fresh, gain], axis=0)

    ns = [noise[0], noise[1]]
    ready = [build(0, 0), build(1, 0)]
    for j in range(steps):
        now = ready
        vs = [ns[h] * now[h][1] + dot_nt(ns[h].astype(bf16), step_ref[h, j]) for h in range(2)]
        if j + 1 < steps:
            ready = [build(0, j + 1), build(1, j + 1)]
        for h in range(2):
            t, decay, decay_t, left, right = now[h]
            e, v = step_ref[h, j], vs[h]
            pushed = dot_nn(jnp.concatenate([e, left], axis=1),
                            jnp.concatenate([v.astype(bf16), right], axis=0))
            n = v * decay_t + base[...] + pushed
            diag[pl.ds(t, 1), :] = jnp.sum(jnp.where(diagonal, n, 0.0), axis=0, keepdims=True)
            ns[h] = n
    for h in range(2):
        noise[h] = ns[h]

    def pairs(maps):
        m01 = product(maps[0], maps[1])
        m23 = product(maps[2], maps[3])
        return m01, m23

    def suffixes(maps, m23):
        later[3] = jnp.where(eye(s), 1.0, 0.0).astype(f32)
        later[2] = maps[3]
        later[1] = m23
        later[0] = product(maps[1], m23)

    def earlier_map(p, maps, m01):
        m012 = product(m01, maps[2])
        unit = jnp.where(eye(s), 1.0, 0.0).astype(f32)
        low = jnp.where(p == 0, unit, maps[0])
        return jnp.where(p < 2, low, jnp.where(p == 2, m01, m012))

    def earlier_part(p, parts, maps):
        p0 = unpack(parts[0])
        p01 = moved(p0, maps[1]) + unpack(parts[1])
        p012 = moved(p01, maps[2]) + unpack(parts[2])
        low = jnp.where(p == 0, 0.0, p0)
        return jnp.where(p < 2, low, jnp.where(p == 2, p01, p012))

    def total_part(ring, p):
        parts = ring.hold
        sum_ = moved(unpack(parts[p]), later[p])
        left, right = ring.neighbours()
        sum_ = sum_ + moved(unpack(parts[left]), later[left])
        sum_ = sum_ + moved(unpack(parts[right]), later[right])
        across = ring.across()
        return pack(sum_ + moved(unpack(parts[across]), later[across]))

    def first_half():
        return jnp.concatenate([noise[0], total_ref[0, s:]], axis=0)

    def second_half():
        return jnp.concatenate([noise[1], total_ref[1, s:]], axis=0)

    @pl.when(jnp.logical_and(i == last, core == 1))
    def _():
        own_part[...] = moved(first_half(), total_ref[1, :s]) + second_half()
        on_chip(own_part, pair_part, 1).start()
        mx.relay()
        before[0] = product(pair_map[...], total_ref[0, :s])
        mx.neighbours()
        mx.across()
        on_chip(map_x, map_x, 3).start()
        x01, x23 = pairs(map_x)
        map_z[z] = product(x01, x23)
        mz.start()
        mz.relay()
        mz.neighbours()
        mz.across()
        on_chip(map_z, map_z, 4).start()
        z01, z23 = pairs(map_z)
        map_y[y] = product(z01, z23)
        my.start()
        on_chip(own_part, pair_part, 1).wait_recv()
        part = pair_part[...]
        kept = moved(part, total_ref[0, :s]) + first_half()
        my.relay()
        my.neighbours()
        my.across()
        on_chip(map_y, map_y, 5).start()
        on_chip(state, state, 2).wait_recv()
        near = unpack(state[...])
        entry[0] = moved(near, pair_map[...]) + pair_part[...]
        entry[1] = moved(near, before[0]) + kept

    @pl.when(jnp.logical_and(i == last, core == 0))
    def _():
        far = product(total_ref[1, :s], pair_map[...])
        mine = moved(first_half(), far) + moved(second_half(), pair_map[...])
        on_chip(own_part, pair_part, 1).wait_recv()
        part_x[x] = pack(mine + pair_part[...])
        px.start()
        own_part[...] = moved(first_half(), total_ref[1, :s]) + second_half()
        on_chip(own_part, pair_part, 1).start()
        px.relay()
        on_chip(map_x, map_x, 3).wait_recv()
        x01, x23 = pairs(map_x)
        suffixes(map_x, x23)
        before[0] = earlier_map(x, map_x, x01)
        part_z[z] = total_part(px, x)
        pz.start()
        near = earlier_part(x, part_x, map_x)
        pz.relay()
        on_chip(map_z, map_z, 4).wait_recv()
        z01, z23 = pairs(map_z)
        suffixes(map_z, z23)
        before[3] = product(earlier_map(z, map_z, z01), before[0])
        part_y[y] = total_part(pz, z)
        py.start()
        near = near + moved(earlier_part(z, part_z, map_z), before[0])
        py.relay()
        on_chip(map_y, map_y, 5).wait_recv()
        for q in (2, 1, 0):
            after = before[q + 1]
            before[q] = jnp.where(q < y, product(map_y[q], after), after)
        t0 = before[0]
        weights = jnp.broadcast_to(var0_ref[...], (8, s)).T[:, 0:1]
        u_hi, u_lo = split(t0)
        w_hi, w_lo = split(t0 * weights)
        u_hi_t, u_lo_t = u_hi.T, u_lo.T
        start_noise = dot_nn(u_hi_t, w_hi) + (dot_nn(u_hi_t, w_lo) + dot_nn(u_lo_t, w_hi))
        start_mean = product(jnp.broadcast_to(mean0_ref[...], (PAD, s)), t0)
        near = near + jnp.concatenate([start_noise, start_mean], axis=0)

        def slab(q):
            part = moved(unpack(part_y[q]), before[jnp.minimum(q + 1, 3)])
            return jnp.where(q < y, part, 0.0)

        left, right = py.neighbours()
        near = near + slab(left) + slab(right)
        near = near + slab(py.across())
        state[...] = pack(near)
        on_chip(state, state, 2).start()
        entry[0] = near
        entry[1] = moved(near, total_ref[0, :s]) + first_half()

    @pl.when(i == last)
    def _():
        for h in range(2):
            cov = entry[h, :s]
            off[h] = jnp.where(diagonal, 0.0, cov).astype(bf16)
            held = jnp.sum(jnp.where(diagonal, cov, 0.0), axis=1, keepdims=True)
            straight[h] = jnp.broadcast_to(held, (s, s))
            first_mean[h] = jnp.broadcast_to(entry[h, s:s + 8].T[:, 0:1], (s, s))
        fetch.wait()

        @pl.loop(0, half // 4)
        def _(block):
            for j in range(4):
                for h in range(2):
                    k = block * 4 + j
                    t = h * half + k
                    maps = maps_here[h, k]
                    r = dot_nn(off[h], maps.astype(bf16)) + straight[h] * maps
                    out_ref[1, pl.ds(t, 1), :] = (
                        jnp.sum(r * maps, axis=0, keepdims=True) + diag[pl.ds(t, 1), :]
                    )
                    out_ref[0, pl.ds(t, 1), :] = (
                        jnp.sum(first_mean[h] * maps, axis=0, keepdims=True)
                        + shift_ref[pl.ds(t, 1), :]
                    )

        on_chip(own_map, pair_map, 0).wait_send()
        on_chip(own_part, pair_part, 1).wait_send()

    @pl.when(jnp.logical_and(i == last, core == 0))
    def _():
        for ring in (px, pz, py):
            ring.drain()
        on_chip(state, state, 2).wait_send()

    @pl.when(jnp.logical_and(i == last, core == 1))
    def _():
        for ring in (mx, mz, my):
            ring.drain()
        for k, hold in ((3, map_x), (4, map_z), (5, map_y)):
            on_chip(hold, hold, k).wait_send()


def scan(decay, obs_var, factor, obs_map, gain, step_maps, total, init_mean, init_var, shift, maps):
    count, s = decay.shape
    m = obs_map.shape[1]
    steps = SPN
    rows = s + PAD
    packed = s // 2 + s // 4 + 8
    block = lambda i: (0, i, 0, 0)
    flat = pl.BlockSpec((2, steps, m, s), block)
    three = lambda i: (0, 0, 0)
    return pl.pallas_call(
        functools.partial(scan_kernel, steps),
        grid=(count // (2 * steps),),
        in_specs=[
            pl.BlockSpec((count, s), whole),
            pl.BlockSpec((1, m), whole),
            pl.BlockSpec((s, s), whole),
            flat,
            flat,
            pl.BlockSpec((2, steps, s, s), block),
            pl.BlockSpec((2, rows, s), three),
            pl.BlockSpec((1, s), whole),
            pl.BlockSpec((1, s), whole),
            pl.BlockSpec((count, s), whole),
            pl.BlockSpec(memory_space=pl.ANY),
        ],
        out_specs=pl.BlockSpec((2, count, s), three),
        out_shape=jax.ShapeDtypeStruct((2, count, s), f32),
        scratch_shapes=[
            pltpu.VMEM((2, s, s), f32),
            pltpu.VMEM((m, 8), f32),
            pltpu.VMEM((s, s), f32),
            pltpu.VMEM((s, s), bf16),
            pltpu.VMEM((count, s), f32),
            pltpu.VMEM((s, s), f32),
            pltpu.VMEM((rows, s), f32),
        ] + [pltpu.VMEM((4, s, s), f32)] * 3 + [pltpu.VMEM((4, packed, s), f32)] * 3 + [
            pltpu.VMEM((4, s, s), f32),
            pltpu.VMEM((4, s, s), f32),
            pltpu.VMEM((s, s), f32),
            pltpu.VMEM((rows, s), f32),
            pltpu.VMEM((packed, s), f32),
            pltpu.VMEM((2, rows, s), f32),
            pltpu.VMEM((2, count // 2, s, s), f32),
            pltpu.VMEM((2, s, s), bf16),
            pltpu.VMEM((2, s, s), f32),
            pltpu.VMEM((2, s, s), f32),
            pltpu.SemaphoreType.DMA((3, 2, 12)),
            pltpu.SemaphoreType.DMA((3, 2, 12)),
            pltpu.SemaphoreType.DMA((2, 6)),
            pltpu.SemaphoreType.DMA((1,)),
        ],
        compiler_params=pltpu.CompilerParams(collective_id=0, has_side_effects=True),
        name="scan_devices",
    )(decay, obs_var[None, :], factor, halves(obs_map), halves(gain), step_maps, total,
      init_mean[None, :], init_var[None, :], shift, maps)


def per_device(
    init_mean, init_var, decay, coupling, obs_map, gain, noise_factor, obs_var, observed
):
    step_maps, maps, shift, total = local_maps(decay, coupling, obs_map, gain, observed)
    both = scan(
        decay, obs_var, noise_factor, obs_map, gain, step_maps, total, init_mean, init_var,
        shift, maps,
    )
    return (both[0], both[1])


def solution(mesh):
    return jax.shard_map(
        per_device,
        mesh=mesh,
        in_specs=(
            P(),
            P(),
            P(("row", "col"), None),
            P(("row", "col"), None, None),
            P(("row", "col"), None, None),
            P(("row", "col"), None, None),
            P(),
            P(),
            P(("row", "col"), None),
        ),
        out_specs=(P(("row", "col"), None), P(("row", "col"), None)),
        check_vma=False,
    )
```

```python
import functools

import jax
import jax.numpy as jnp
from jax import lax
from jax.experimental import pallas as pl
from jax.experimental.pallas import tpu as pltpu
from jax.sharding import PartitionSpec as P

f32 = jnp.float32
bf16 = jnp.bfloat16
PAD = 16
SPB = 4
SPN = 8


def dot_nn(a, b):
    return lax.dot_general(a, b, (((1,), (0,)), ((), ())), preferred_element_type=f32)


def dot_nt(a, b):
    return lax.dot_general(a, b, (((1,), (1,)), ((), ())), preferred_element_type=f32)


def split(x):
    hi = x.astype(bf16)
    return hi, (x - hi.astype(f32)).astype(bf16)


def eye(n):
    row = lax.broadcasted_iota(jnp.int32, (n, n), 0)
    col = lax.broadcasted_iota(jnp.int32, (n, n), 1)
    return row == col


MESH_ID = pl.DeviceIdType.MESH


def product(a, b):
    a_hi, a_lo = split(a)
    b_hi, b_lo = split(b)
    return dot_nn(a_hi, b_hi) + (dot_nn(a_lo, b_hi) + dot_nn(a_hi, b_lo))


def moved(part, maps):
    s = maps.shape[0]
    t_hi, t_lo = split(maps)
    x_hi, x_lo = split(part)
    y = dot_nn(x_hi, t_hi) + (dot_nn(x_lo, t_hi) + dot_nn(x_hi, t_lo))
    v_hi, v_lo = split(y[:s])
    u_hi, u_lo = t_hi.T, t_lo.T
    n = dot_nn(u_hi, v_hi) + (dot_nn(u_hi, v_lo) + dot_nn(u_lo, v_hi))
    return jnp.concatenate([n, y[s:]], axis=0)


def pack(part):
    s = part.shape[1]
    h, k = s // 2, s // 4
    square = jnp.concatenate([part[h:h + k, h:], part[h + k:s, h:]], axis=1)
    return jnp.concatenate([part[:h], square, part[s:s + 8]], axis=0)


def unpack(packed):
    s = packed.shape[1]
    h, k = s // 2, s // 4
    top, square, shift = packed[:h], packed[h:h + k], packed[h + k:]
    corner = jnp.concatenate([square[:, :h], square[:, h:]], axis=0)
    low = jnp.concatenate([top[:, h:].T, corner], axis=1)
    return jnp.concatenate([top, low] + [shift] * (PAD // 8), axis=0)


def maps_kernel(steps, decay_ref, observed_ref, coupling_ref, map_ref, gain_ref,
                step_ref, maps_ref, shift_ref, total_ref, own_ref, state):
    i = pl.program_id(0)
    s = decay_ref.shape[1]
    half = decay_ref.shape[0] // 2

    @pl.when(i == 0)
    def _():
        unit = jnp.where(eye(s), 1.0, 0.0).astype(f32)
        for h in range(2):
            state[h] = jnp.concatenate([unit, jnp.zeros((PAD, s), f32)], axis=0)

    def build(h, j):
        t = h * half + i * steps + j
        decay = decay_ref[pl.ds(t, 1), :]
        obs_map, gain, coupling = map_ref[h, j], gain_ref[h, j], coupling_ref[h, j]
        obs_f = (obs_map.astype(f32) * decay + dot_nn(obs_map, coupling)).astype(bf16)
        e_hi, e_lo = split(coupling.astype(f32) - dot_nn(gain.T, obs_f))
        step_ref[h, j] = e_hi
        z_hi, z_lo = split(jnp.broadcast_to(observed_ref[pl.ds(t, 1), :], (PAD, gain.shape[0])))
        both = dot_nn(jnp.concatenate([z_hi, z_lo], axis=0), gain)
        return t, decay, e_hi, e_lo, both[:PAD] + both[PAD:]

    diagonal = eye(s)
    maps = [state[0], state[1]]
    ready = [build(0, 0), build(1, 0)]
    for j in range(steps):
        for h in range(2):
            t, decay, e_hi, e_lo, shift = ready[h]
            m_hi, m_lo = split(maps[h])
            moved = dot_nt(jnp.concatenate([m_hi, m_lo], axis=0), e_hi)
            y = maps[h] * decay + (moved[:s + PAD] + (moved[s + PAD:] + dot_nt(m_hi, e_lo)))
            b = y[s:] + shift
            maps_ref[h, j] = y[:s]
            own_ref[pl.ds(t, 1), :] = jnp.sum(jnp.where(diagonal, y[:s], 0.0), axis=0, keepdims=True)
            shift_ref[pl.ds(t, 1), :] = b[0:1]
            maps[h] = jnp.concatenate([y[:s], b], axis=0)
            if j + 1 < steps:
                ready[h] = build(h, j + 1)
    for h in range(2):
        state[h] = maps[h]

    @pl.when(i == pl.num_programs(0) - 1)
    def _():
        total_ref[...] = state[...]


def halves(a):
    return a.reshape((2, a.shape[0] // 2) + a.shape[1:])


def whole(i):
    return (0, 0)


def local_maps(decay, coupling, obs_map, gain, observed):
    count, s = decay.shape
    m = obs_map.shape[1]
    steps = SPB
    block = lambda i: (0, i, 0, 0)
    square = pl.BlockSpec((2, steps, s, s), block)
    flat = pl.BlockSpec((2, steps, m, s), block)
    return pl.pallas_call(
        functools.partial(maps_kernel, steps),
        grid=(count // (2 * steps),),
        in_specs=[pl.BlockSpec((count, s), whole), pl.BlockSpec((count, m), whole),
                  square, flat, flat],
        out_specs=[square, square, pl.BlockSpec((count, s), whole),
                   pl.BlockSpec((2, s + PAD, s), lambda i: (0, 0, 0)),
                   pl.BlockSpec((count, s), whole)],
        out_shape=[
            jax.ShapeDtypeStruct((2, count // 2, s, s), bf16),
            jax.ShapeDtypeStruct((2, count // 2, s, s), f32),
            jax.ShapeDtypeStruct((count, s), f32),
            jax.ShapeDtypeStruct((2, s + PAD, s), f32),
            jax.ShapeDtypeStruct((count, s), f32),
        ],
        scratch_shapes=[pltpu.VMEM((2, s + PAD, s), f32)],
        name="local_maps",
    )(decay, observed, halves(coupling), halves(obs_map), halves(gain))


def scan_kernel(steps, decay_ref, var_ref, factor_ref, map_ref, gain_ref, step_ref, total_ref,
                mean0_ref, var0_ref, shift_ref, own_ref, maps_ref, out_ref,
                noise, obs_var, base, base_half, diag, own_map, own_part,
                map_x, map_z, map_y, part_x, part_z, part_y,
                later, before, pair_map, pair_part, state, entry, maps_here, cov_half,
                first_mean, send_sem, recv_sem, pair_sem, maps_sem):
    i = pl.program_id(0)
    last = pl.num_programs(0) - 1
    row, col = lax.axis_index("row"), lax.axis_index("col")
    y, z = row // 4, lax.rem(row, 4)
    x, core = col // 2, lax.rem(col, 2)
    s = decay_ref.shape[1]
    half = decay_ref.shape[0] // 2

    def step(p, by):
        return lax.rem(p + by, 4)

    def along_x(by):
        return (row, step(x, by) * 2 + core)

    def along_z(by):
        return (y * 4 + step(z, by), col)

    def along_y(by):
        return (step(y, by) * 4 + z, col)

    partner = (row, x * 2 + 1 - core)

    def on_chip(source, target, k):
        return pltpu.make_async_remote_copy(
            src_ref=source, dst_ref=target, send_sem=pair_sem.at[0, k],
            recv_sem=pair_sem.at[1, k], device_id=partner, device_id_type=MESH_ID)

    class Ring:
        def __init__(self, level, kind, hold, p, along):
            self.sem, self.hold, self.p = (level, kind), hold, p
            self.right, self.left = along(1), along(3)
            rows = hold.shape[1]
            q = rows // 32 * 8
            self.cut = [(0, rows - 3 * q)] + [(rows - k * q, q) for k in (3, 2, 1)]

        def piece(self, source, k, sem, target):
            rows = pl.ds(*self.cut[k])
            slot = step(self.p, source)
            return pltpu.make_async_remote_copy(
                src_ref=self.hold.at[slot, rows], dst_ref=self.hold.at[slot, rows],
                send_sem=send_sem.at[(*self.sem, sem)], recv_sem=recv_sem.at[(*self.sem, sem)],
                device_id=target, device_id_type=MESH_ID)

        def start(self):
            for k in range(4):
                self.piece(0, k, k, self.right).start()
                other = (k + 2) % 4
                self.piece(0, other, 4 + other, self.left).start()

        def relay(self):
            for k in range(2):
                self.piece(3, k, k, self.right).wait_recv()
                self.piece(3, k, 8 + k, self.right).start()
                self.piece(1, k + 2, 6 + k, self.left).wait_recv()
                self.piece(1, k + 2, 10 + k, self.left).start()

        def neighbours(self):
            for k in range(2):
                self.piece(3, k + 2, k + 2, self.right).wait_recv()
                self.piece(1, k, 4 + k, self.left).wait_recv()
            return step(self.p, 3), step(self.p, 1)

        def across(self):
            for k in range(2):
                self.piece(2, k, 8 + k, self.right).wait_recv()
                self.piece(2, k + 2, 10 + k, self.left).wait_recv()
            return step(self.p, 2)

        def drain(self):
            for k in range(4):
                self.piece(0, k, k, self.right).wait_send()
                self.piece(0, k, 4 + k, self.left).wait_send()
            for k in range(2):
                self.piece(3, k, 8 + k, self.right).wait_send()
                self.piece(1, k + 2, 10 + k, self.left).wait_send()

    mx, px = Ring(0, 0, map_x, x, along_x), Ring(0, 1, part_x, x, along_x)
    mz, pz = Ring(1, 0, map_z, z, along_z), Ring(1, 1, part_z, z, along_z)
    my, py = Ring(2, 0, map_y, y, along_y), Ring(2, 1, part_y, y, along_y)

    @pl.when(i == 0)
    def _():
        barrier = pltpu.get_barrier_semaphore()
        pl.semaphore_signal(barrier, inc=1, device_id=partner, device_id_type=MESH_ID)
        for along in (along_x, along_z, along_y):
            for by in (1, 3):
                pl.semaphore_signal(barrier, inc=1, device_id=along(by), device_id_type=MESH_ID)
        noise[...] = jnp.zeros_like(noise)
        obs_var[...] = jnp.broadcast_to(var_ref[...] * 0.5, obs_var.shape[::-1]).T
        own_map[...] = product(total_ref[0, :s], total_ref[1, :s])
        q = dot_nt(factor_ref[...], factor_ref[...])
        base[...] = q
        base_half[...] = q.astype(bf16)
        pl.semaphore_wait(barrier, 7)
        on_chip(own_map, pair_map, 0).start()

    fetch = pltpu.make_async_copy(maps_ref, maps_here, maps_sem.at[0])

    @pl.when(i == 1)
    def _():
        fetch.start()
        on_chip(own_map, pair_map, 0).wait_recv()

    @pl.when(jnp.logical_and(i == 1, core == 1))
    def _():
        map_x[x] = product(pair_map[...], own_map[...])
        mx.start()

    diagonal = eye(s)
    m = map_ref.shape[2]
    seen_all = dot_nn(map_ref[...].reshape(-1, s), base_half[...])

    def build(h, j):
        t = h * half + i * steps + j
        k = h * steps + j
        obs_map, gain = map_ref[h, j], gain_ref[h, j]
        seen = seen_all[k * m:(k + 1) * m]
        inner = (dot_nt(obs_map, seen.astype(bf16)) * 0.5).astype(bf16)
        fresh = (dot_nn(inner, gain) + gain.astype(f32) * obs_var[:, 0:1] - seen).astype(bf16)
        decay = decay_ref[pl.ds(t, 1), :]
        decay_t = jnp.broadcast_to(decay, (8, s)).T[:, 0:1]
        left = jnp.concatenate([gain, fresh], axis=0).T
        return t, decay, decay_t, left, jnp.concatenate([fresh, gain], axis=0)

    ns = [noise[0], noise[1]]
    ready = [build(0, 0), build(1, 0)]
    for j in range(steps):
        now = ready
        vs = [ns[h] * now[h][1] + dot_nt(ns[h].astype(bf16), step_ref[h, j]) for h in range(2)]
        if j + 1 < steps:
            ready = [build(0, j + 1), build(1, j + 1)]
        for h in range(2):
            t, decay, decay_t, left, right = now[h]
            e, v = step_ref[h, j], vs[h]
            pushed = dot_nn(jnp.concatenate([e, left], axis=1),
                            jnp.concatenate([v.astype(bf16), right], axis=0))
            n = v * decay_t + base[...] + pushed
            diag[pl.ds(t, 1), :] = jnp.sum(jnp.where(diagonal, n, 0.0), axis=0, keepdims=True)
            ns[h] = n
    for h in range(2):
        noise[h] = ns[h]

    def pairs(maps):
        m01 = product(maps[0], maps[1])
        m23 = product(maps[2], maps[3])
        return m01, m23

    def suffixes(maps, m23):
        later[3] = jnp.where(eye(s), 1.0, 0.0).astype(f32)
        later[2] = maps[3]
        later[1] = m23
        later[0] = product(maps[1], m23)

    def earlier_map(p, maps, m01):
        m012 = product(m01, maps[2])
        unit = jnp.where(eye(s), 1.0, 0.0).astype(f32)
        low = jnp.where(p == 0, unit, maps[0])
        return jnp.where(p < 2, low, jnp.where(p == 2, m01, m012))

    def earlier_part(p, parts, maps):
        p0 = unpack(parts[0])
        p01 = moved(p0, maps[1]) + unpack(parts[1])
        p012 = moved(p01, maps[2]) + unpack(parts[2])
        low = jnp.where(p == 0, 0.0, p0)
        return jnp.where(p < 2, low, jnp.where(p == 2, p01, p012))

    def total_part(ring, p):
        parts = ring.hold
        sum_ = moved(unpack(parts[p]), later[p])
        left, right = ring.neighbours()
        sum_ = sum_ + moved(unpack(parts[left]), later[left])
        sum_ = sum_ + moved(unpack(parts[right]), later[right])
        across = ring.across()
        return pack(sum_ + moved(unpack(parts[across]), later[across]))

    def first_half():
        return jnp.concatenate([noise[0], total_ref[0, s:]], axis=0)

    def second_half():
        return jnp.concatenate([noise[1], total_ref[1, s:]], axis=0)

    @pl.when(jnp.logical_and(i == last, core == 1))
    def _():
        own_part[...] = moved(first_half(), total_ref[1, :s]) + second_half()
        on_chip(own_part, pair_part, 1).start()
        mx.relay()
        before[0] = product(pair_map[...], total_ref[0, :s])
        mx.neighbours()
        mx.across()
        on_chip(map_x, map_x, 3).start()
        x01, x23 = pairs(map_x)
        map_z[z] = product(x01, x23)
        mz.start()
        mz.relay()
        mz.neighbours()
        mz.across()
        on_chip(map_z, map_z, 4).start()
        z01, z23 = pairs(map_z)
        map_y[y] = product(z01, z23)
        my.start()
        on_chip(own_part, pair_part, 1).wait_recv()
        part = pair_part[...]
        kept = moved(part, total_ref[0, :s]) + first_half()
        my.relay()
        my.neighbours()
        my.across()
        on_chip(map_y, map_y, 5).start()
        on_chip(state, state, 2).wait_recv()
        near = unpack(state[...])
        entry[0] = moved(near, pair_map[...]) + pair_part[...]
        entry[1] = moved(near, before[0]) + kept

    @pl.when(jnp.logical_and(i == last, core == 0))
    def _():
        far = product(total_ref[1, :s], pair_map[...])
        mine = moved(first_half(), far) + moved(second_half(), pair_map[...])
        on_chip(own_part, pair_part, 1).wait_recv()
        part_x[x] = pack(mine + pair_part[...])
        px.start()
        own_part[...] = moved(first_half(), total_ref[1, :s]) + second_half()
        on_chip(own_part, pair_part, 1).start()
        px.relay()
        on_chip(map_x, map_x, 3).wait_recv()
        x01, x23 = pairs(map_x)
        suffixes(map_x, x23)
        before[0] = earlier_map(x, map_x, x01)
        part_z[z] = total_part(px, x)
        pz.start()
        near = earlier_part(x, part_x, map_x)
        pz.relay()
        on_chip(map_z, map_z, 4).wait_recv()
        z01, z23 = pairs(map_z)
        suffixes(map_z, z23)
        before[3] = product(earlier_map(z, map_z, z01), before[0])
        part_y[y] = total_part(pz, z)
        py.start()
        near = near + moved(earlier_part(z, part_z, map_z), before[0])
        py.relay()
        on_chip(map_y, map_y, 5).wait_recv()
        for q in (2, 1, 0):
            after = before[q + 1]
            before[q] = jnp.where(q < y, product(map_y[q], after), after)
        t0 = before[0]
        weights = jnp.broadcast_to(var0_ref[...], (8, s)).T[:, 0:1]
        u_hi, u_lo = split(t0)
        w_hi, w_lo = split(t0 * weights)
        u_hi_t, u_lo_t = u_hi.T, u_lo.T
        start_noise = dot_nn(u_hi_t, w_hi) + (dot_nn(u_hi_t, w_lo) + dot_nn(u_lo_t, w_hi))
        start_mean = product(jnp.broadcast_to(mean0_ref[...], (PAD, s)), t0)
        near = near + jnp.concatenate([start_noise, start_mean], axis=0)

        def slab(q):
            part = moved(unpack(part_y[q]), before[jnp.minimum(q + 1, 3)])
            return jnp.where(q < y, part, 0.0)

        left, right = py.neighbours()
        near = near + slab(left) + slab(right)
        near = near + slab(py.across())
        state[...] = pack(near)
        on_chip(state, state, 2).start()
        entry[0] = near
        entry[1] = moved(near, total_ref[0, :s]) + first_half()

    @pl.when(i == last)
    def _():
        firsts = []
        for h in range(2):
            cov, mean = entry[h, :s], entry[h, s:]
            held = jnp.sum(jnp.where(diagonal, cov, 0.0), axis=0, keepdims=True)
            cov_half[h] = cov.astype(bf16)
            first_mean[h] = jnp.broadcast_to(mean[:8].T[:, 0:1], (s, s))
            firsts.append((held, held.astype(bf16).astype(f32)))
        fetch.wait()

        @pl.loop(0, half // 4)
        def _(block):
            for j in range(4):
                for h in range(2):
                    k = block * 4 + j
                    t = h * half + k
                    maps = maps_here[h, k]
                    near_maps = maps.astype(bf16)
                    r = dot_nn(cov_half[h], near_maps)
                    held, held_hi = firsts[h]
                    own = own_ref[pl.ds(t, 1), :]
                    own_hi = own.astype(bf16).astype(f32)
                    out_ref[1, pl.ds(t, 1), :] = (
                        jnp.sum(r * maps, axis=0, keepdims=True)
                        + own * (held * own - held_hi * own_hi) + diag[pl.ds(t, 1), :]
                    )
                    out_ref[0, pl.ds(t, 1), :] = (
                        jnp.sum(first_mean[h] * maps, axis=0, keepdims=True)
                        + shift_ref[pl.ds(t, 1), :]
                    )

        on_chip(own_map, pair_map, 0).wait_send()
        on_chip(own_part, pair_part, 1).wait_send()

    @pl.when(jnp.logical_and(i == last, core == 0))
    def _():
        for ring in (px, pz, py):
            ring.drain()
        on_chip(state, state, 2).wait_send()

    @pl.when(jnp.logical_and(i == last, core == 1))
    def _():
        for ring in (mx, mz, my):
            ring.drain()
        for k, hold in ((3, map_x), (4, map_z), (5, map_y)):
            on_chip(hold, hold, k).wait_send()


def scan(decay, obs_var, factor, obs_map, gain, step_maps, total, init_mean, init_var, shift, own,
         maps):
    count, s = decay.shape
    m = obs_map.shape[1]
    steps = SPN
    rows = s + PAD
    packed = s // 2 + s // 4 + 8
    block = lambda i: (0, i, 0, 0)
    flat = pl.BlockSpec((2, steps, m, s), block)
    three = lambda i: (0, 0, 0)
    return pl.pallas_call(
        functools.partial(scan_kernel, steps),
        grid=(count // (2 * steps),),
        in_specs=[
            pl.BlockSpec((count, s), whole),
            pl.BlockSpec((1, m), whole),
            pl.BlockSpec((s, s), whole),
            flat,
            flat,
            pl.BlockSpec((2, steps, s, s), block),
            pl.BlockSpec((2, rows, s), three),
            pl.BlockSpec((1, s), whole),
            pl.BlockSpec((1, s), whole),
            pl.BlockSpec((count, s), whole),
            pl.BlockSpec((count, s), whole),
            pl.BlockSpec(memory_space=pl.ANY),
        ],
        out_specs=pl.BlockSpec((2, count, s), three),
        out_shape=jax.ShapeDtypeStruct((2, count, s), f32),
        scratch_shapes=[
            pltpu.VMEM((2, s, s), f32),
            pltpu.VMEM((m, 8), f32),
            pltpu.VMEM((s, s), f32),
            pltpu.VMEM((s, s), bf16),
            pltpu.VMEM((count, s), f32),
            pltpu.VMEM((s, s), f32),
            pltpu.VMEM((rows, s), f32),
        ] + [pltpu.VMEM((4, s, s), f32)] * 3 + [pltpu.VMEM((4, packed, s), f32)] * 3 + [
            pltpu.VMEM((4, s, s), f32),
            pltpu.VMEM((4, s, s), f32),
            pltpu.VMEM((s, s), f32),
            pltpu.VMEM((rows, s), f32),
            pltpu.VMEM((packed, s), f32),
            pltpu.VMEM((2, rows, s), f32),
            pltpu.VMEM((2, count // 2, s, s), f32),
            pltpu.VMEM((2, s, s), bf16),
            pltpu.VMEM((2, s, s), f32),
            pltpu.SemaphoreType.DMA((3, 2, 12)),
            pltpu.SemaphoreType.DMA((3, 2, 12)),
            pltpu.SemaphoreType.DMA((2, 6)),
            pltpu.SemaphoreType.DMA((1,)),
        ],
        compiler_params=pltpu.CompilerParams(collective_id=0, has_side_effects=True),
        name="scan_devices",
    )(decay, obs_var[None, :], factor, halves(obs_map), halves(gain), step_maps, total,
      init_mean[None, :], init_var[None, :], shift, own, maps)


def per_device(
    init_mean, init_var, decay, coupling, obs_map, gain, noise_factor, obs_var, observed
):
    step_maps, maps, shift, total, own = local_maps(decay, coupling, obs_map, gain, observed)
    both = scan(
        decay, obs_var, noise_factor, obs_map, gain, step_maps, total, init_mean, init_var,
        shift, own, maps,
    )
    return (both[0], both[1])


def solution(mesh):
    return jax.shard_map(
        per_device,
        mesh=mesh,
        in_specs=(
            P(),
            P(),
            P(("row", "col"), None),
            P(("row", "col"), None, None),
            P(("row", "col"), None, None),
            P(("row", "col"), None, None),
            P(),
            P(),
            P(("row", "col"), None),
        ),
        out_specs=(P(("row", "col"), None), P(("row", "col"), None)),
        check_vma=False,
    )
```
